32 devices in a mesh: groups: 2 (over x), row: 8 (over z, y), col: 2 (over core).
Axes of the slice: x: 2, y: 2, z: 4, core: 2. Of those that a mesh axis runs over, the one named last changes fastest.
Arguments:
- features: bfloat16 [32, 8, 256, 1024], P(('groups', 'row'), 'col'), parts along dimension 0, may hold values from -6 to 6
- assignment: int32 [32, 8], P(('groups', 'row'), 'col'), parts along dimension 0, may hold values from -1 to 7, as said below
- w_reduce: bfloat16 [1024, 512], replicated, may hold values from -0.1875 to 0.1875
- w_expand: bfloat16 [512, 2048], replicated, may hold values from -0.25 to 0.25
- w_short: bfloat16 [1024, 2048], replicated, may hold values from -0.1875 to 0.1875
- w_branch: bfloat16 [2048, 256], replicated, may hold values from -0.125 to 0.125
- w_dilated: bfloat16 [9, 256, 256], replicated, may hold values from -0.125 to 0.125
Outputs:
- branch_out: bfloat16 [512, 128, 256], P(('groups', 'row'), 'col'), parts along dimension 0
The draws below stay inside these ranges and needn't reach their ends.
There are 2 independent parts, one for each index of `groups`. The reference program is written for one: setup_inputs(seed, part) draws one part's arguments, and reference() takes and returns one part's arrays. A program takes and returns all parts, laid end to end along the dimension named above; an argument that names none is the same for every part. Nothing has to cross between parts.
Inputs may be any that keep to these rules, and one draw needn't show every extreme that they name: `assignment`: A value v >= 0 means the tile has tissue and is handled in slot v % 4 by the worker of the same column index whose row index is the holder's row index XOR (v // 4): the holder itself for v < 4, else its partner. Each worker handles exactly 4 tiles, one in each slot, the holder's own tissue tiles included. In every column index some device's tiles are all tissue, so that it hands 4 tiles to its partner, and that partner holds none.
All inputs are finite; a program needn't handle non-finite values.
Results may differ from the reference program's by a relative error of at most 0.0061.
Values may be sent and summed in bfloat16 or wider, within the bound.
No kernel may reach another device: no remote copies, remote signals or barrier semaphores. Data moves between devices by JAX's collectives and lax.ppermute only.
A program may use at most 64 MiB of HBM per device.

```python
import jax
import jax.numpy as jnp
from jax import lax

CIN = 1024
MID = 512
COUT = 2048
BR = 256
TILE = 16
TRD = 2
TCD = 4
RR = 18
RC = 15
LOAD = 4
TR = 16
TC = 8
N_ROW = 8
N_COL = 2


def draw_assignment(key, part):
    tile_count = TRD * TCD
    pair_count = N_ROW // 2
    spread = jax.random.randint(jax.random.fold_in(key, 11), (N_COL, pair_count), (LOAD + 1) // 2, LOAD + 1)
    spread = spread.at[:, 0].set(LOAD)
    flipped = jax.random.randint(jax.random.fold_in(key, 14), (N_COL, pair_count), 0, 2)
    higher = LOAD + spread
    lower = LOAD - spread
    even_count = jnp.where(flipped == 0, higher, lower)
    odd_count = jnp.where(flipped == 0, lower, higher)
    counts = jnp.stack([even_count, odd_count], axis=-1).reshape(N_COL, N_ROW)
    partner_counts = jnp.stack([odd_count, even_count], axis=-1).reshape(N_COL, N_ROW)
    rank_keys = jax.random.split(jax.random.fold_in(key, 13), N_COL * N_ROW)
    tile_ranks = jax.vmap(lambda single: jax.random.permutation(single, tile_count))(rank_keys)
    tile_ranks = tile_ranks.reshape(N_COL, N_ROW, tile_count).astype(jnp.int32)
    slot_keys = jax.random.split(jax.random.fold_in(key, 15), N_COL * N_ROW)
    slot_perms = jax.vmap(lambda single: jax.random.permutation(single, LOAD))(slot_keys)
    slot_perms = slot_perms.reshape(N_COL, N_ROW, LOAD).astype(jnp.int32)
    partner_perms = slot_perms.reshape(N_COL, pair_count, 2, LOAD)[:, :, ::-1, :].reshape(N_COL, N_ROW, LOAD)
    tissue = tile_ranks < counts[:, :, None]
    handed = tile_ranks >= LOAD
    base_slot = jnp.where(handed, partner_counts[:, :, None] + tile_ranks - LOAD, tile_ranks)
    base_slot = jnp.clip(base_slot, 0, LOAD - 1).astype(jnp.int32)
    own_slot = jnp.take_along_axis(slot_perms, base_slot, axis=2)
    other_slot = jnp.take_along_axis(partner_perms, base_slot, axis=2)
    slot_index = jnp.where(handed, other_slot, own_slot)
    values = jnp.where(tissue, handed.astype(jnp.int32) * LOAD + slot_index, -1).astype(jnp.int32)
    values = values.reshape(N_COL, N_ROW, TRD, TCD).transpose(1, 2, 0, 3)
    return values.reshape(TRD * N_ROW, TCD * N_COL)


def steps_of(key, extent, cuts, low, high):
    level, own = 1.0, jax.random.fold_in(key, 6)
    for axis_at, parts in cuts:
        draws = jnp.exp(jax.random.uniform(jax.random.fold_in(own, axis_at), (parts,), jnp.float32, low / len(cuts), high / len(cuts)))
        level = level * jnp.repeat(draws, extent[axis_at] // parts).reshape([-1 if axis == axis_at else 1 for axis in range(len(extent))])
    return level


def bell_draw(key, extent, scale, most, cuts=(), held_as=jnp.bfloat16):
    level = steps_of(key, extent, cuts, -0.22, 0.18) if cuts else 1.0
    result = jax.random.normal(key, extent, jnp.float32) * scale * level
    return jnp.minimum(jnp.maximum(result, -most), most).astype(held_as)


def setup_inputs(seed: int = 0, part: int = 0) -> dict:
    keys = jax.random.split(jax.random.key(seed), 8)
    part_splits = jax.random.split(jax.random.fold_in(keys[7], part), 8)
    features = bell_draw(part_splits[0], (TR, TC, TILE * TILE, CIN), 1.0, 6.0, ((0, 8), (1, 2)))
    assignment = draw_assignment(jax.random.fold_in(jax.random.fold_in(keys[7], part), 71), part)
    w_reduce = bell_draw(keys[2], (CIN, MID), CIN ** -0.5, 0.1875)
    w_expand = bell_draw(keys[3], (MID, COUT), MID ** -0.5, 0.25)
    w_short = bell_draw(keys[4], (CIN, COUT), CIN ** -0.5, 0.1875)
    w_branch = bell_draw(keys[5], (COUT, BR), COUT ** -0.5, 0.125)
    w_dilated = bell_draw(keys[6], (9, BR, BR), (9 * BR) ** -0.5, 0.125)
    return {"features": features, "assignment": assignment, "w_reduce": w_reduce, "w_expand": w_expand, "w_short": w_short, "w_branch": w_branch, "w_dilated": w_dilated}


def trunk(rows_in, w_reduce, w_expand, w_short, w_branch):
    hidden = jax.nn.relu(jnp.dot(rows_in, w_reduce, preferred_element_type=jnp.float32)).astype(jnp.bfloat16)
    summed = jnp.dot(hidden, w_expand, preferred_element_type=jnp.float32) + jnp.dot(rows_in, w_short, preferred_element_type=jnp.float32)
    block_out = jax.nn.relu(summed).astype(jnp.bfloat16)
    return jax.nn.relu(jnp.dot(block_out, w_branch, preferred_element_type=jnp.float32)).astype(jnp.bfloat16)


def reference(features, assignment, w_reduce, w_expand, w_short, w_branch, w_dilated):
    pixels = TILE * TILE
    tissue_count = N_ROW * N_COL * LOAD
    flat_in = features.reshape(TR * TC, pixels, CIN)
    tissue = assignment.reshape(TR * TC) >= 0
    chosen = jnp.nonzero(tissue, size=tissue_count)[0].astype(jnp.int32)
    picked = flat_in[chosen].reshape(tissue_count // LOAD, LOAD * pixels, CIN)

    def one_block(rows_in):
        return trunk(rows_in, w_reduce, w_expand, w_short, w_branch)

    reduced = lax.map(one_block, picked).reshape(tissue_count, pixels, BR)
    tile_grid = jnp.zeros((TR * TC, pixels, BR), jnp.bfloat16).at[chosen].set(reduced)
    height = TR * TILE
    width = TC * TILE
    feature_grid = tile_grid.reshape(TR, TC, TILE, TILE, BR).transpose(0, 2, 1, 3, 4).reshape(height, width, BR)
    padded = jnp.pad(feature_grid, ((RR, RR), (RC, RC), (0, 0)))
    summed = jnp.zeros((height * width, BR), jnp.float32)
    for down_tap in range(3):
        for side_tap in range(3):
            window = padded[down_tap * RR:down_tap * RR + height, side_tap * RC:side_tap * RC + width]
            summed = summed + jnp.dot(window.reshape(height * width, BR), w_dilated[3 * down_tap + side_tap], preferred_element_type=jnp.float32)
    return jax.nn.relu(summed).astype(jnp.bfloat16).reshape(height, width, BR)
```

```python
import functools

import jax
import jax.numpy as jnp
from jax import lax
from jax.experimental import pallas as pl
from jax.experimental.pallas import tpu as pltpu
from jax.sharding import PartitionSpec as P


TILE = 16
RR = 18
RC = 15
F32 = jnp.float32
BF16 = jnp.bfloat16
VM = pl.BlockSpec(memory_space=pltpu.VMEM)
SM = pl.BlockSpec(memory_space=pltpu.SMEM)
HBM = pl.BlockSpec(memory_space=pltpu.MemorySpace.HBM)
MIB = 1 << 20
TRUNK_MIB = 16


def params(mib):
    return pltpu.CompilerParams(vmem_limit_bytes=mib * MIB)


def cost(flops, nbytes):
    return pl.CostEstimate(flops=int(flops), bytes_accessed=int(nbytes), transcendentals=0)


def pieces_of(cols, top, tile_rows):
    found = []
    for tr in range(tile_rows):
        first, last = tr * TILE, (tr + 1) * TILE
        lo, hi = (first, min(last, RR)) if top else (max(first, RR), last)
        if hi > lo:
            found += [(tr, tc, lo - first, hi - lo) for tc in cols]
    return found


def trunk_rows(x, wr, we, ws, wb, ready):
    block = 512
    ready(0)
    hidden = jnp.maximum(jnp.dot(x, wr[...], preferred_element_type=F32), 0).astype(BF16)
    total = None
    for k, at in enumerate(range(0, we.shape[1], block)):
        ready(1 + k)
        summed = jnp.dot(hidden, we[:, at : at + block], preferred_element_type=F32)
        summed = summed + jnp.dot(x, ws[:, at : at + block], preferred_element_type=F32)
        block_out = jnp.maximum(summed, 0).astype(BF16)
        term = jnp.dot(block_out, wb[at : at + block, :], preferred_element_type=F32)
        total = term if total is None else total + term
    return jnp.maximum(total, 0)


def put_rows(reduced, pieces, cols, row_base, flags, out):
    at = 0
    for tr, tc, first, count in pieces:
        part = reduced[at : at + count * TILE]
        part = jnp.where(flags[tr, tc] >= 0, part, 0.0).astype(BF16)
        where = cols.index(tc) * TILE
        start = tr * TILE + first - row_base
        out[start : start + count, where : where + TILE, :] = part.reshape(count, TILE, part.shape[-1])
        at += count * TILE


def first_chunk(chunks, cols, flags, feats, wr_h, we_h, ws_h, wb_h, out, xs, wr, we, ws, wb, sems):
    block = 512
    copies = []

    def go(src, dst):
        copy = pltpu.make_async_copy(src, dst, sems.at[len(copies)])
        copy.start()
        copies.append(copy)

    at = 0
    spans = []
    for pieces in chunks:
        start = len(copies)
        for tr, tc, first, count in pieces:
            go(feats.at[tr, tc, pl.ds(first * TILE, count * TILE), :], xs.at[pl.ds(at, count * TILE), :])
            at += count * TILE
        spans.append((start, len(copies)))
        if len(spans) == 1:
            groups = [[len(copies)]]
            go(wr_h, wr)
            for k in range(0, we.shape[1], block):
                groups.append([len(copies) + j for j in range(3)])
                go(we_h.at[:, pl.ds(k, block)], we.at[:, pl.ds(k, block)])
                go(ws_h.at[:, pl.ds(k, block)], ws.at[:, pl.ds(k, block)])
                go(wb_h.at[pl.ds(k, block), :], wb.at[pl.ds(k, block), :])

    def ready(k):
        for j in groups[k]:
            copies[j].wait()

    for j in range(*spans[0]):
        copies[j].wait()
    rows = sum(p[3] for p in chunks[0]) * TILE
    reduced = trunk_rows(xs[0:rows, :], wr, we, ws, wb, ready)
    put_rows(reduced, chunks[0], cols, 0, flags, out)
    for span in spans[1:]:
        for j in range(*span):
            copies[j].wait()


def later_chunk(pieces, cols, at, top, flags, xs, wr, we, ws, wb, *refs):
    out = refs[-1]
    rows = sum(p[3] for p in pieces) * TILE
    reduced = trunk_rows(xs[at : at + rows, :], wr, we, ws, wb, lambda k: None)
    base = 0 if top else out_base(out)
    put_rows(reduced, pieces, cols, base, flags, out)
    if not top:
        head = refs[0]
        out[0 : RR - base, :, :] = head[base:RR, :, :]


def out_base(out):
    return 2 * TILE - out.shape[0]


def conv_kernel(flags, w, te, be, tm, bm, hte, hbe, htm, hbm_, xs, out, ext):
    rows, width = out.shape[0], out.shape[1]
    br = w.shape[1]
    base = rows - RR
    n_edge = te.shape[1] // 2

    def lay(at, count, src_e, src_m, first):
        ext[at : at + count, TILE : TILE + n_edge, :] = src_e[first : first + count, 0:n_edge, :]
        ext[at : at + count, TILE + n_edge : TILE + width - n_edge, :] = src_m[first : first + count, :, :]
        ext[at : at + count, TILE + width - n_edge : TILE + width, :] = src_e[first : first + count, n_edge:, :]

    lay(0, RR, hte, htm, 0)
    lay(RR, RR, te, tm, 0)
    lay(2 * RR, rows - RR, be, bm, RR - base)
    lay(RR + rows, RR, hbe, hbm_, 0)

    zero = jnp.zeros((rows + 2 * RR, TILE, br), BF16)
    for side, at in ((0, 0), (1, TILE + width)):
        @pl.when(flags[side] != 0)
        def _():
            ext[0:RR, at : at + TILE, :] = xs[0:RR]
            ext[RR : 2 * RR, at : at + TILE, :] = xs[RR : 2 * RR]
            ext[2 * RR : RR + rows, at : at + TILE, :] = xs[2 * RR + RR - base : 3 * RR]
            ext[RR + rows :, at : at + TILE, :] = xs[3 * RR : 4 * RR]

        @pl.when(flags[side] == 0)
        def _():
            ext[:, at : at + TILE, :] = zero

    step = 8
    for r in range(0, rows, step):
        total = None
        for a in range(3):
            for b in range(3):
                left = TILE - RC + b * RC
                window = ext[r + a * RR : r + a * RR + step, left : left + width, :]
                term = jnp.dot(window.reshape(step * width, br), w[3 * a + b], preferred_element_type=F32)
                total = term if total is None else total + term
        out[r : r + step] = jnp.maximum(total, 0).astype(BF16).reshape(step, width, br)


def shards(features, assignment, w_reduce, w_expand, w_short, w_branch, w_dilated):
    tile_rows, tile_cols, _, channels = features.shape
    mid, cout, br = w_reduce.shape[1], w_expand.shape[1], w_branch.shape[1]
    height, width = tile_rows * TILE, tile_cols * TILE
    edge = [0, tile_cols - 1]
    middle = list(range(1, tile_cols - 1))
    sets = [(edge, True), (edge, False), (middle, True), (middle, False)]
    chunks = [pieces_of(cols, top, tile_rows) for cols, top in sets]
    sizes = [sum(p[3] for p in c) * TILE for c in chunks]
    starts = [sum(sizes[:i]) for i in range(len(sizes))]
    per_row = 2 * (channels * mid + mid * cout + channels * cout + cout * br)
    n_copies = sum(len(c) for c in chunks) + 1 + 3 * (cout // 512)

    def grid_of(cols):
        return jax.ShapeDtypeStruct((RR, len(cols) * TILE, br), BF16)

    te, xs, wr, we, ws, wb = pl.pallas_call(
        functools.partial(first_chunk, chunks, edge),
        out_shape=[
            grid_of(edge),
            jax.ShapeDtypeStruct((sum(sizes), channels), BF16),
            jax.ShapeDtypeStruct(w_reduce.shape, BF16),
            jax.ShapeDtypeStruct(w_expand.shape, BF16),
            jax.ShapeDtypeStruct(w_short.shape, BF16),
            jax.ShapeDtypeStruct(w_branch.shape, BF16),
        ],
        in_specs=[SM] + [HBM] * 5,
        out_specs=[VM] * 6,
        scratch_shapes=[pltpu.SemaphoreType.DMA((n_copies,))],
        compiler_params=params(TRUNK_MIB),
        cost_estimate=cost(per_row * sizes[0], 12 * MIB),
        name="trunk_first",
    )(
        assignment,
        *[
            pltpu.with_memory_space_constraint(v, pltpu.MemorySpace.HBM)
            for v in (features, w_reduce, w_expand, w_short, w_branch)
        ],
    )

    def later(i, *extra):
        cols, top = sets[i]
        return pl.pallas_call(
            functools.partial(later_chunk, chunks[i], cols, starts[i], top),
            out_shape=grid_of(cols),
            in_specs=[SM] + [VM] * (5 + len(extra)),
            out_specs=VM,
            compiler_params=params(TRUNK_MIB),
            cost_estimate=cost(per_row * sizes[i], MIB),
        )(assignment, xs, wr, we, ws, wb, *extra)

    rows_n = lax.axis_size("row")
    up = [(i + 1, i) for i in range(rows_n - 1)]
    down = [(i, i + 1) for i in range(rows_n - 1)]

    hbe = lax.ppermute(te, "row", up)
    be = later(1, te)
    hte = lax.ppermute(be, "row", down)
    tm = later(2)
    hbm_ = lax.ppermute(tm, "row", up)
    bm = later(3, tm)
    htm = lax.ppermute(bm, "row", down)

    cols_n = lax.axis_size("col")
    me = lax.axis_index("col")
    half = len(edge) * TILE // 2
    mine = jnp.concatenate([hte, te, be, hbe], axis=0)
    sent = jnp.where(me == 0, mine[:, half:], mine[:, :half])
    xside = lax.ppermute(sent, "col", [(0, 1), (1, 0)])
    flags = jnp.stack([me > 0, me < cols_n - 1]).astype(jnp.int32)

    return pl.pallas_call(
        conv_kernel,
        out_shape=jax.ShapeDtypeStruct((height, width, br), BF16),
        in_specs=[SM] + [VM] * 10,
        out_specs=VM,
        scratch_shapes=[pltpu.VMEM((height + 2 * RR, width + 2 * TILE, br), BF16)],
        compiler_params=params(24),
        cost_estimate=cost(2 * height * width * 9 * br * br, 6 * MIB),
        name="dilated",
    )(flags, w_dilated, te, be, tm, bm, hte, hbe, htm, hbm_, xside)


def solution(mesh):
    in_specs = (
        P(("groups", "row"), "col", None, None),
        P(("groups", "row"), "col"),
        P(),
        P(),
        P(),
        P(),
        P(),
    )
    out_specs = P(("groups", "row"), "col", None)

    return jax.shard_map(shards, mesh=mesh, in_specs=in_specs, out_specs=out_specs, check_vma=False)
```

```python
import functools

import jax
import jax.numpy as jnp
from jax import lax
from jax.experimental import pallas as pl
from jax.experimental.pallas import tpu as pltpu
from jax.sharding import PartitionSpec as P


TILE = 16
RR = 18
RC = 15
BLOCK = 512
F32 = jnp.float32
BF16 = jnp.bfloat16
VM = pl.BlockSpec(memory_space=pltpu.VMEM)
SM = pl.BlockSpec(memory_space=pltpu.SMEM)
HBM = pl.BlockSpec(memory_space=pltpu.MemorySpace.HBM)
MIB = 1 << 20
TRUNK_MIB = 16
CONV_MIB = 24


def params(mib):
    return pltpu.CompilerParams(vmem_limit_bytes=mib * MIB)


def cost(flops, nbytes):
    return pl.CostEstimate(flops=int(flops), bytes_accessed=int(nbytes), transcendentals=0)


def in_hbm(value):
    return pltpu.with_memory_space_constraint(value, pltpu.MemorySpace.HBM)


def near_is_top():
    return lax.rem(lax.axis_index("row"), 2)


def columns_of(chunk):
    return chunk[0]


def span(chunk, height):
    return (RR if chunk[1] else height - RR) * TILE


def sources(chunk, top):
    rest = (RR - TILE) * TILE
    pixels = TILE * TILE
    for j, col in enumerate(chunk[0]):
        if chunk[1]:
            at = j * (pixels + rest)
            yield 1 - top, col, 0, pixels, at
            yield top, col, (1 - top) * (pixels - rest), rest, at + pixels
        else:
            yield top, col, top * rest, pixels - rest, j * (pixels - rest)


def trunk_rows(x, wr, we, ws, wb, ready=lambda k: None):
    ready(0)
    hidden = jnp.maximum(jnp.dot(x, wr[...], preferred_element_type=F32), 0).astype(BF16)
    total = None
    for k, at in enumerate(range(0, we.shape[1], BLOCK)):
        ready(1 + k)
        summed = jnp.dot(hidden, we[:, at : at + BLOCK], preferred_element_type=F32)
        summed = summed + jnp.dot(x, ws[:, at : at + BLOCK], preferred_element_type=F32)
        block_out = jnp.maximum(summed, 0).astype(BF16)
        term = jnp.dot(block_out, wb[at : at + BLOCK, :], preferred_element_type=F32)
        total = term if total is None else total + term
    return jnp.maximum(total, 0)


def put_column(part, chunk, col, j, top, flags, out):
    width = part.shape[-1]
    where = pl.ds(j * TILE, TILE)
    own = flags[top, col] >= 0
    if chunk[1]:
        pixels = TILE * TILE
        full = jnp.where(flags[1 - top, col] >= 0, part[:pixels], 0.0).astype(BF16)
        rest = jnp.where(own, part[pixels:], 0.0).astype(BF16)
        out[pl.ds((1 - top) * (RR - TILE), TILE), where, :] = full.reshape(TILE, TILE, width)
        out[pl.ds(top * TILE, RR - TILE), where, :] = rest.reshape(RR - TILE, TILE, width)
    else:
        rows = part.shape[0] // TILE
        part = jnp.where(own, part, 0.0).astype(BF16)
        out[pl.ds(top * (RR - rows), rows), where, :] = part.reshape(rows, TILE, width)


def first_chunk(chunks, height, asg, feats, wr_h, we_h, ws_h, wb_h, out, xs, wr, we, ws, wb, flags, sems):
    top = near_is_top()
    steps = [[]]
    steps[0].append((asg, flags))
    at = 0
    later = []
    for i, chunk in enumerate(chunks):
        moves = [
            (feats.at[tr, col, pl.ds(first, count), :], xs.at[pl.ds(at + row, count), :])
            for tr, col, first, count, row in sources(chunk, top)
        ]
        at += span(chunk, height) * len(columns_of(chunk))
        if i == 0:
            steps[0] += moves
        else:
            later.append(moves)
    steps[0].append((wr_h, wr))
    for k in range(0, we.shape[1], BLOCK):
        cols = pl.ds(k, BLOCK)
        steps.append(
            [(ws_h.at[:, cols], ws.at[:, cols]), (we_h.at[:, cols], we.at[:, cols]), (wb_h.at[cols, :], wb.at[cols, :])]
        )
    n_weights = len(steps)
    steps += later
    copies = []
    used = 0
    for step in steps:
        copies.append([pltpu.make_async_copy(src, dst, sems.at[used + j]) for j, (src, dst) in enumerate(step)])
        used += len(step)

    def begin(k):
        if k < len(copies):
            for copy in copies[k]:
                copy.start()

    def ready(k):
        for copy in copies[k]:
            copy.wait()
        begin(k + 2)

    begin(0)
    begin(1)
    ready(0)
    per = span(chunks[0], height)
    cols = columns_of(chunks[0])
    reduced = trunk_rows(xs[0 : per * len(cols), :], wr, we, ws, wb, lambda k: ready(k) if k else None)
    for j, col in enumerate(cols):
        put_column(reduced[j * per : (j + 1) * per], chunks[0], col, j, top, flags, out)
    for k in range(n_weights, len(copies)):
        ready(k)


def later_chunk(chunk, at, height, flags, xs, wr, we, ws, wb, *refs):
    out = refs[-1]
    top = near_is_top()
    per = span(chunk, height)
    cols = columns_of(chunk)

    def busy(col):
        own = flags[top, col] >= 0
        if chunk[1]:
            own = own | (flags[1 - top, col] >= 0)
        return own

    active = [busy(col) for col in cols]
    every = functools.reduce(lambda a, b: a & b, active)
    zero = jnp.zeros((span(chunk, height), out.shape[-1]), F32)

    @pl.when(every)
    def _():
        reduced = trunk_rows(xs[at : at + per * len(cols), :], wr, we, ws, wb)
        for j, col in enumerate(cols):
            put_column(reduced[j * per : (j + 1) * per], chunk, col, j, top, flags, out)

    if len(cols) == 1:
        @pl.when(jnp.logical_not(every))
        def _():
            put_column(zero, chunk, cols[0], 0, top, flags, out)
    else:
        for j, col in enumerate(cols):
            @pl.when(jnp.logical_not(active[j]))
            def _():
                put_column(zero, chunk, col, j, top, flags, out)

        one = cols[0]
        step = cols[1] - cols[0]

        @pl.loop(0, len(cols))
        def _(j):
            col = one + j * step
            mine = flags[top, col] >= 0
            if chunk[1]:
                mine = mine | (flags[1 - top, col] >= 0)

            @pl.when(mine & jnp.logical_not(every))
            def _():
                rows = pl.ds(pl.multiple_of(at + j * per, TILE), per)
                put_column(trunk_rows(xs[rows, :], wr, we, ws, wb), chunk, col, j, top, flags, out)

    if not chunk[1]:
        near = refs[0]
        shared = 2 * RR - height
        out[pl.ds((1 - top) * (RR - shared), shared)] = near[pl.ds(top * (RR - shared), shared)]


def pick_kernel(cols_n, *refs):
    n = 1 if cols_n == 2 else 2
    ins, outs = refs[:-n], refs[-n:]
    width = ins[0].shape[1]
    for i, src in enumerate(ins):
        rows = pl.ds(i * RR, RR)
        if cols_n == 2:
            first = pl.multiple_of((1 - lax.axis_index("col")) * (width - TILE), TILE)
            outs[0][rows] = src[:, pl.ds(first, TILE), :]
        else:
            outs[0][rows] = src[:, width - TILE :, :]
            outs[1][rows] = src[:, :TILE, :]


def lay_columns(groups, width, cols_n, row, count, src, first, side, side_row, sides, ext):
    rows = pl.ds(row, count)
    taken = pl.ds(first, count)
    for cols, ref in zip(groups, src):
        for j, col in enumerate(cols):
            ext[rows, (1 + col) * TILE : (2 + col) * TILE, :] = ref[taken, j * TILE : (j + 1) * TILE, :]
    me = lax.axis_index("col")
    zero = jnp.zeros((count, TILE, ext.shape[-1]), BF16)
    for on, at, ref in ((me > 0, 0, sides[0]), (me < cols_n - 1, TILE + width, sides[-1])):
        there = ref[pl.ds(side * RR + side_row, count)]
        ext[rows, at : at + TILE, :] = jnp.where(on, there, zero)


def spread(ext, cat, width):
    br = ext.shape[-1]
    for b in range(3):
        left = TILE - RC + b * RC
        cat[:, :, b * br : (b + 1) * br] = ext[:, left : left + width, :]


def conv_early(groups, cols_n, height, w, *refs):
    g = len(groups)
    near, far, halo = refs[:g], refs[g : 2 * g], refs[2 * g : 3 * g]
    sides = refs[3 * g : -6]
    out, partial, ext, cat, done, sem = refs[-6:]
    top = near_is_top()
    width = cat.shape[1]
    br = ext.shape[-1]
    rest = height - RR
    lay = functools.partial(lay_columns, groups, width, cols_n)
    local = top * RR
    lay((1 - top) * height, RR, halo, 0, 2, 0, sides, ext)
    lay(local + (1 - top) * rest, RR, near, 0, 0, 0, sides, ext)
    far_row = top * (RR - rest)
    lay(local + top * RR, rest, far, far_row, 1, far_row, sides, ext)
    spread(ext, cat, width)
    k = 3 * br
    total = None
    for a in range(3):
        term = jnp.dot(
            cat[a * RR : a * RR + rest].reshape(rest * width, k), w[a * k : (a + 1) * k, :], preferred_element_type=F32
        )
        total = term if total is None else total + term
    done[...] = jnp.maximum(total, 0).astype(BF16).reshape(rest, width, br)
    copy = pltpu.make_async_copy(done, out.at[pl.ds((1 - top) * RR, rest)], sem)
    copy.start()
    centre = cat[pl.ds(top * height, RR)].reshape(RR * width, k)
    inner = cat[pl.ds(top * rest + (1 - top) * RR, RR)].reshape(RR * width, k)
    inner_w = w[pl.ds(pl.multiple_of((1 - top) * 2 * k, k), k), :]
    partial[...] = jnp.dot(centre, w[k : 2 * k, :], preferred_element_type=F32) + jnp.dot(
        inner, inner_w, preferred_element_type=F32
    )
    copy.wait()


def conv_late(groups, cols_n, height, w, partial, *refs):
    g = len(groups)
    halo = refs[:g]
    sides = refs[g:-6]
    _, out, ext, cat, done, sem = refs[-6:]
    top = near_is_top()
    width = cat.shape[1]
    br = ext.shape[-1]
    lay_columns(groups, width, cols_n, 0, RR, halo, 0, 3, 0, sides, ext)
    spread(ext, cat, width)
    k = 3 * br
    outer_w = w[pl.ds(pl.multiple_of(top * 2 * k, k), k), :]
    total = partial[...] + jnp.dot(cat[...].reshape(RR * width, k), outer_w, preferred_element_type=F32)
    done[...] = jnp.maximum(total, 0).astype(BF16).reshape(RR, width, br)
    copy = pltpu.make_async_copy(done, out.at[pl.ds(top * (height - RR), RR)], sem)
    copy.start()
    copy.wait()


def plan(tile_cols):
    groups = [[0, tile_cols - 1], list(range(1, tile_cols - 1))]
    order = [(i, near) for i in range(len(groups)) for near in (True, False)]
    return groups, order


def shards(features, assignment, w_reduce, w_expand, w_short, w_branch, w_dilated):
    tile_rows, tile_cols, pixels, channels = features.shape
    mid, cout, br = w_reduce.shape[1], w_expand.shape[1], w_branch.shape[1]
    height, width = tile_rows * TILE, tile_cols * TILE
    assert tile_rows == 2 and pixels == TILE * TILE and TILE < RR <= height <= 2 * RR
    groups, order = plan(tile_cols)
    chunks = [(groups[i], near) for i, near in order]
    sizes = [span(c, height) * len(c[0]) for c in chunks]
    starts = [sum(sizes[:i]) for i in range(len(sizes))]
    per_row = 2 * (channels * mid + mid * cout + channels * cout + cout * br)
    n_copies = sum(len(list(sources(c, 0))) for c in chunks) + 2 + 3 * (cout // BLOCK)

    def grid_of(cols):
        return jax.ShapeDtypeStruct((RR, len(cols) * TILE, br), BF16)

    first, xs, wr, we, ws, wb = pl.pallas_call(
        functools.partial(first_chunk, chunks, height),
        out_shape=[
            grid_of(chunks[0][0]),
            jax.ShapeDtypeStruct((sum(sizes), channels), BF16),
            jax.ShapeDtypeStruct(w_reduce.shape, BF16),
            jax.ShapeDtypeStruct(w_expand.shape, BF16),
            jax.ShapeDtypeStruct(w_short.shape, BF16),
            jax.ShapeDtypeStruct(w_branch.shape, BF16),
        ],
        in_specs=[HBM] * 6,
        out_specs=[VM] * 6,
        scratch_shapes=[pltpu.SMEM(assignment.shape, jnp.int32), pltpu.SemaphoreType.DMA((n_copies,))],
        compiler_params=params(TRUNK_MIB),
        cost_estimate=cost(per_row * sizes[0], 12 * MIB),
        name="trunk_first",
    )(*[in_hbm(v) for v in (assignment, features, w_reduce, w_expand, w_short, w_branch)])

    rows_n = lax.axis_size("row")
    swap = [(i, i ^ 1) for i in range(rows_n) if i ^ 1 < rows_n]
    cross = [pair for i in range(1, rows_n - 1, 2) for pair in ((i, i + 1), (i + 1, i))]

    local, halo = {}, {}
    for n, (i, near) in enumerate(order):
        if n == 0:
            value = first
        else:
            extra = [] if near else [local[i, True]]
            value = pl.pallas_call(
                functools.partial(later_chunk, chunks[n], starts[n], height),
                out_shape=grid_of(groups[i]),
                in_specs=[SM] + [VM] * (5 + len(extra)),
                out_specs=VM,
                compiler_params=params(TRUNK_MIB),
                cost_estimate=cost(per_row * sizes[n], MIB),
            )(assignment, xs, wr, we, ws, wb, *extra)
        local[i, near] = value
        halo[i, near] = lax.ppermute(value, "row", swap if near else cross)

    cols_n = lax.axis_size("col")
    side = jax.ShapeDtypeStruct((4 * RR, TILE, br), BF16)
    one_swap = cols_n == 2
    picked = pl.pallas_call(
        functools.partial(pick_kernel, cols_n),
        out_shape=[side] if one_swap else [side, side],
        in_specs=[VM] * 4,
        out_specs=[VM] * (1 if one_swap else 2),
        compiler_params=params(4),
        cost_estimate=cost(0, MIB),
        name="pick",
    )(local[0, True], local[0, False], halo[0, True], halo[0, False])
    if one_swap:
        sides = [lax.ppermute(picked[0], "col", [(0, 1), (1, 0)])]
    else:
        sides = [
            lax.ppermute(picked[0], "col", [(i, i + 1) for i in range(cols_n - 1)]),
            lax.ppermute(picked[1], "col", [(i + 1, i) for i in range(cols_n - 1)]),
        ]

    taps = w_dilated.reshape(9 * br, br)
    rest = height - RR
    n_groups = len(groups)
    pick = lambda table, near: [table[i, near] for i in range(n_groups)]
    flops = 2 * width * 3 * br * br
    out, partial = pl.pallas_call(
        functools.partial(conv_early, groups, cols_n, height),
        out_shape=[
            jax.ShapeDtypeStruct((height, width, br), BF16),
            jax.ShapeDtypeStruct((RR * width, br), F32),
        ],
        in_specs=[VM] * (1 + 3 * n_groups + len(sides)),
        out_specs=[HBM, VM],
        scratch_shapes=[
            pltpu.VMEM((height + RR, width + 2 * TILE, br), BF16),
            pltpu.VMEM((height + RR, width, 3 * br), BF16),
            pltpu.VMEM((rest, width, br), BF16),
            pltpu.SemaphoreType.DMA,
        ],
        compiler_params=params(CONV_MIB),
        cost_estimate=cost(flops * (3 * rest + 2 * RR), 4 * MIB),
        name="conv_early",
    )(taps, *pick(local, True), *pick(local, False), *pick(halo, True), *sides)
    n_in = 2 + n_groups + len(sides)
    return pl.pallas_call(
        functools.partial(conv_late, groups, cols_n, height),
        out_shape=jax.ShapeDtypeStruct((height, width, br), BF16),
        in_specs=[VM] * n_in + [HBM],
        out_specs=HBM,
        input_output_aliases={n_in: 0},
        scratch_shapes=[
            pltpu.VMEM((RR, width + 2 * TILE, br), BF16),
            pltpu.VMEM((RR, width, 3 * br), BF16),
            pltpu.VMEM((RR, width, br), BF16),
            pltpu.SemaphoreType.DMA,
        ],
        compiler_params=params(16),
        cost_estimate=cost(flops * RR, 2 * MIB),
        name="conv_late",
    )(taps, partial, *pick(halo, False), *sides, out)


def solution(mesh):
    in_specs = (
        P(("groups", "row"), "col", None, None),
        P(("groups", "row"), "col"),
        P(),
        P(),
        P(),
        P(),
        P(),
    )
    out_specs = P(("groups", "row"), "col", None)

    return jax.shard_map(shards, mesh=mesh, in_specs=in_specs, out_specs=out_specs, check_vma=False)
```

```python
import functools

import jax
import jax.numpy as jnp
from jax import lax
from jax.experimental import pallas as pl
from jax.experimental.pallas import tpu as pltpu
from jax.sharding import PartitionSpec as P


TILE = 16
RR = 18
RC = 15
BLOCK = 512
DEPTH = 3
LATE = 3
F32 = jnp.float32
BF16 = jnp.bfloat16
VM = pl.BlockSpec(memory_space=pltpu.VMEM)
SM = pl.BlockSpec(memory_space=pltpu.SMEM)
HBM = pl.BlockSpec(memory_space=pltpu.MemorySpace.HBM)
MIB = 1 << 20
TRUNK_MIB = 16
CONV_MIB = 24


def params(mib):
    return pltpu.CompilerParams(vmem_limit_bytes=mib * MIB)


def cost(flops, nbytes):
    return pl.CostEstimate(flops=int(flops), bytes_accessed=int(nbytes), transcendentals=0)


def in_hbm(value):
    return pltpu.with_memory_space_constraint(value, pltpu.MemorySpace.HBM)


def near_is_top():
    return lax.rem(lax.axis_index("row"), 2)


def top_of(near_first):
    return near_is_top() if near_first else 1 - near_is_top()


def columns_of(chunk):
    return chunk[0]


def span(chunk, height):
    return (RR if chunk[1] else height - RR) * TILE


def sources(chunk, top):
    rest = (RR - TILE) * TILE
    pixels = TILE * TILE
    for j, col in enumerate(chunk[0]):
        if chunk[1]:
            at = j * (pixels + rest)
            yield 1 - top, col, 0, pixels, at
            yield top, col, (1 - top) * (pixels - rest), rest, at + pixels
        else:
            yield top, col, top * rest, pixels - rest, j * (pixels - rest)


def trunk_rows(x, wr, we, ws, wb, ready=lambda k: None):
    ready(0)
    hidden = jnp.maximum(jnp.dot(x, wr[...], preferred_element_type=F32), 0).astype(BF16)
    total = None
    for k, at in enumerate(range(0, we.shape[1], BLOCK)):
        ready(1 + k)
        summed = jnp.dot(hidden, we[:, at : at + BLOCK], preferred_element_type=F32)
        summed = summed + jnp.dot(x, ws[:, at : at + BLOCK], preferred_element_type=F32)
        block_out = jnp.maximum(summed, 0).astype(BF16)
        term = jnp.dot(block_out, wb[at : at + BLOCK, :], preferred_element_type=F32)
        total = term if total is None else total + term
    return jnp.maximum(total, 0)


def put_column(part, chunk, col, j, top, flags, out):
    width = part.shape[-1]
    where = pl.ds(j * TILE, TILE)
    own = flags[top, col] >= 0
    if chunk[1]:
        pixels = TILE * TILE
        full = jnp.where(flags[1 - top, col] >= 0, part[:pixels], 0.0).astype(BF16)
        rest = jnp.where(own, part[pixels:], 0.0).astype(BF16)
        out[pl.ds((1 - top) * (RR - TILE), TILE), where, :] = full.reshape(TILE, TILE, width)
        out[pl.ds(top * TILE, RR - TILE), where, :] = rest.reshape(RR - TILE, TILE, width)
    else:
        rows = part.shape[0] // TILE
        part = jnp.where(own, part, 0.0).astype(BF16)
        out[pl.ds(top * (RR - rows), rows), where, :] = part.reshape(rows, TILE, width)


def first_chunk(chunks, height, asg, feats, wr_h, we_h, ws_h, wb_h, out, xs, wr, we, ws, wb, flags, sems):
    steps = [[]]
    steps[0].append((asg, flags))
    at = 0
    later = []
    for i, chunk in enumerate(chunks):
        moves = [
            (feats.at[tr, col, pl.ds(first, count), :], xs.at[pl.ds(at + row, count), :])
            for tr, col, first, count, row in sources(chunk, top_of(chunk[2]))
        ]
        at += span(chunk, height) * len(columns_of(chunk))
        if i == 0:
            steps[0] += moves
        else:
            later += moves
    steps[0].append((wr_h, wr))
    for k in range(0, we.shape[1], BLOCK):
        cols = pl.ds(k, BLOCK)
        steps.append(
            [(ws_h.at[:, cols], ws.at[:, cols]), (we_h.at[:, cols], we.at[:, cols]), (wb_h.at[cols, :], wb.at[cols, :])]
        )
    n_weights = len(steps)
    steps.append(later)
    copies = []
    used = 0
    for step in steps:
        copies.append([pltpu.make_async_copy(src, dst, sems.at[used + j]) for j, (src, dst) in enumerate(step)])
        used += len(step)

    def begin(k):
        if k < len(copies):
            for copy in copies[k]:
                copy.start()

    def ready(k):
        for copy in copies[k]:
            copy.wait()
        begin(k + DEPTH)

    for k in range(DEPTH):
        begin(k)
    ready(0)
    per = span(chunks[0], height)
    cols = columns_of(chunks[0])
    reduced = trunk_rows(xs[0 : per * len(cols), :], wr, we, ws, wb, lambda k: ready(k) if k else None)
    for j, col in enumerate(cols):
        put_column(reduced[j * per : (j + 1) * per], chunks[0], col, j, top_of(chunks[0][2]), flags, out)
    for k in range(n_weights, len(copies)):
        ready(k)


def later_chunk(chunk, at, height, flags, xs, wr, we, ws, wb, *refs):
    out = refs[-1]
    top = top_of(chunk[2])
    per = span(chunk, height)
    cols = columns_of(chunk)

    def busy(col):
        own = flags[top, col] >= 0
        if chunk[1]:
            own = own | (flags[1 - top, col] >= 0)
        return own

    active = [busy(col) for col in cols]
    every = functools.reduce(lambda a, b: a & b, active)
    zero = jnp.zeros((span(chunk, height), out.shape[-1]), F32)

    @pl.when(every)
    def _():
        reduced = trunk_rows(xs[at : at + per * len(cols), :], wr, we, ws, wb)
        for j, col in enumerate(cols):
            put_column(reduced[j * per : (j + 1) * per], chunk, col, j, top, flags, out)

    if len(cols) == 1:
        @pl.when(jnp.logical_not(every))
        def _():
            put_column(zero, chunk, cols[0], 0, top, flags, out)
    else:
        for j, col in enumerate(cols):
            @pl.when(jnp.logical_not(active[j]))
            def _():
                put_column(zero, chunk, col, j, top, flags, out)

        one = cols[0]
        step = cols[1] - cols[0]

        @pl.loop(0, len(cols))
        def _(j):
            col = one + j * step
            mine = flags[top, col] >= 0
            if chunk[1]:
                mine = mine | (flags[1 - top, col] >= 0)

            @pl.when(mine & jnp.logical_not(every))
            def _():
                rows = pl.ds(pl.multiple_of(at + j * per, TILE), per)
                put_column(trunk_rows(xs[rows, :], wr, we, ws, wb), chunk, col, j, top, flags, out)

    if not chunk[1]:
        near = refs[0]
        shared = 2 * RR - height
        out[pl.ds((1 - top) * (RR - shared), shared)] = near[pl.ds(top * (RR - shared), shared)]


def pick_kernel(cols_n, *refs):
    n = 1 if cols_n == 2 else 2
    ins, outs = refs[:-n], refs[-n:]
    width = ins[0].shape[1]
    for i, src in enumerate(ins):
        rows = pl.ds(i * RR, RR)
        if cols_n == 2:
            first = pl.multiple_of((1 - lax.axis_index("col")) * (width - TILE), TILE)
            outs[0][rows] = src[:, pl.ds(first, TILE), :]
        else:
            outs[0][rows] = src[:, width - TILE :, :]
            outs[1][rows] = src[:, :TILE, :]


def place(cols, src, first, count, ext, row):
    for j, col in enumerate(cols):
        ext[pl.ds(row, count), (1 + col) * TILE : (2 + col) * TILE, :] = src[
            pl.ds(first, count), j * TILE : (j + 1) * TILE, :
        ]


def place_sides(cols_n, sides, part, first, count, ext, row):
    me = lax.axis_index("col")
    wide = ext.shape[1]
    for on, at, ref in ((me > 0, 0, sides[0]), (me < cols_n - 1, wide - TILE, sides[-1])):
        there = ref[pl.ds(part * RR + first, count)]
        ext[pl.ds(row, count), at : at + TILE, :] = jnp.where(on, there, jnp.zeros_like(there))


def spread(ext, cat, width):
    br = ext.shape[-1]
    for b in range(3):
        left = TILE - RC + b * RC
        cat[:, :, b * br : (b + 1) * br] = ext[:, left : left + width, :]


def conv_early(groups, cols_n, height, w, *refs):
    g = len(groups)
    ones, twos, halo = refs[:g], refs[g : 2 * g], refs[2 * g : 3 * g]
    sides = refs[3 * g : -6]
    out, partial, ext, cat, done, sem = refs[-6:]
    top = near_is_top()
    width = cat.shape[1]
    rest = height - RR
    local = top * RR
    for i, (cols, near_first) in enumerate(groups):
        up = top_of(near_first)
        skip = up * (RR - rest)
        rows = ((0, ones[i], 0, RR, local + (1 - up) * rest), (1, twos[i], skip, rest, local + up * RR))
        rows += ((2, halo[i], 0, RR, (1 - top) * height),)
        for part, src, first, count, row in rows:
            place(cols, src, first, count, ext, row)
            if i == 0:
                place_sides(cols_n, sides, part, first, count, ext, row)
    spread(ext, cat, width)
    k = cat.shape[2]
    total = None
    for a in range(3):
        term = jnp.dot(
            cat[a * RR : a * RR + rest].reshape(rest * width, k), w[a * k : (a + 1) * k, :], preferred_element_type=F32
        )
        total = term if total is None else total + term
    done[...] = jnp.maximum(total, 0).astype(BF16).reshape(done.shape)
    copy = pltpu.make_async_copy(done, out.at[pl.ds((1 - top) * RR, rest)], sem)
    copy.start()
    centre = cat[pl.ds(top * height, RR)].reshape(RR * width, k)
    inner = cat[pl.ds(top * rest + (1 - top) * RR, RR)].reshape(RR * width, k)
    inner_w = w[pl.ds(pl.multiple_of((1 - top) * 2 * k, k), k), :]
    partial[...] = jnp.dot(centre, w[k : 2 * k, :], preferred_element_type=F32) + jnp.dot(
        inner, inner_w, preferred_element_type=F32
    )
    copy.wait()


def conv_late(groups, cols_n, height, w, partial, *refs):
    g = len(groups)
    halo = refs[:g]
    sides = refs[g:-6]
    _, out, ext, cat, done, sems = refs[-6:]
    top = near_is_top()
    width = cat.shape[1]
    for i, (cols, _) in enumerate(groups):
        place(cols, halo[i], 0, RR, ext, 0)
    place_sides(cols_n, sides, 3, 0, RR, ext, 0)
    spread(ext, cat, width)
    k = cat.shape[2]
    outer_w = w[pl.ds(pl.multiple_of(top * 2 * k, k), k), :]
    step = RR // LATE
    copies = []
    for n in range(LATE):
        at = n * step
        taps = cat[at : at + step].reshape(step * width, k)
        total = partial[at * width : (at + step) * width, :] + jnp.dot(taps, outer_w, preferred_element_type=F32)
        done[at : at + step] = jnp.maximum(total, 0).astype(BF16).reshape(step, width, done.shape[2])
        there = out.at[pl.ds(top * (height - RR) + at, step)]
        copies.append(pltpu.make_async_copy(done.at[pl.ds(at, step)], there, sems.at[n]))
        copies[-1].start()
    for copy in copies:
        copy.wait()


def plan(tile_cols):
    groups = [([0, tile_cols - 1], False), (list(range(1, tile_cols - 1)), True)]
    order = [(0, True), (0, False), (1, True), (1, False)]
    return groups, order


def shards(features, assignment, w_reduce, w_expand, w_short, w_branch, w_dilated):
    tile_rows, tile_cols, pixels, channels = features.shape
    mid, cout, br = w_reduce.shape[1], w_expand.shape[1], w_branch.shape[1]
    height, width = tile_rows * TILE, tile_cols * TILE
    assert tile_rows == 2 and pixels == TILE * TILE and TILE < RR <= height <= 2 * RR
    groups, order = plan(tile_cols)
    chunks = [(groups[i][0], one, groups[i][1]) for i, one in order]
    sizes = [span(c, height) * len(c[0]) for c in chunks]
    starts = [sum(sizes[:i]) for i in range(len(sizes))]
    per_row = 2 * (channels * mid + mid * cout + channels * cout + cout * br)
    n_copies = sum(len(list(sources(c, 0))) for c in chunks) + 2 + 3 * (cout // BLOCK)

    def grid_of(cols):
        return jax.ShapeDtypeStruct((RR, len(cols) * TILE, br), BF16)

    first, xs, wr, we, ws, wb = pl.pallas_call(
        functools.partial(first_chunk, chunks, height),
        out_shape=[
            grid_of(chunks[0][0]),
            jax.ShapeDtypeStruct((sum(sizes), channels), BF16),
            jax.ShapeDtypeStruct(w_reduce.shape, BF16),
            jax.ShapeDtypeStruct(w_expand.shape, BF16),
            jax.ShapeDtypeStruct(w_short.shape, BF16),
            jax.ShapeDtypeStruct(w_branch.shape, BF16),
        ],
        in_specs=[HBM] * 6,
        out_specs=[VM] * 6,
        scratch_shapes=[pltpu.SMEM(assignment.shape, jnp.int32), pltpu.SemaphoreType.DMA((n_copies,))],
        compiler_params=params(TRUNK_MIB),
        cost_estimate=cost(per_row * sizes[0], 12 * MIB),
        name="trunk_first",
    )(*[in_hbm(v) for v in (assignment, features, w_reduce, w_expand, w_short, w_branch)])

    rows_n = lax.axis_size("row")
    swap = [(i, i ^ 1) for i in range(rows_n) if i ^ 1 < rows_n]
    cross = [pair for i in range(1, rows_n - 1, 2) for pair in ((i, i + 1), (i + 1, i))]

    local, halo = {}, {}
    for n, (i, one) in enumerate(order):
        if n == 0:
            value = first
        else:
            extra = [] if one else [local[i, True]]
            value = pl.pallas_call(
                functools.partial(later_chunk, chunks[n], starts[n], height),
                out_shape=grid_of(groups[i][0]),
                in_specs=[SM] + [VM] * (5 + len(extra)),
                out_specs=VM,
                compiler_params=params(TRUNK_MIB),
                cost_estimate=cost(per_row * sizes[n], MIB),
            )(assignment, xs, wr, we, ws, wb, *extra)
        local[i, one] = value
        near = one == groups[i][1]
        halo[i, near] = lax.ppermute(value, "row", swap if near else cross)

    cols_n = lax.axis_size("col")
    side = jax.ShapeDtypeStruct((4 * RR, TILE, br), BF16)
    one_swap = cols_n == 2
    picked = pl.pallas_call(
        functools.partial(pick_kernel, cols_n),
        out_shape=[side] if one_swap else [side, side],
        in_specs=[VM] * 4,
        out_specs=[VM] * (1 if one_swap else 2),
        compiler_params=params(4),
        cost_estimate=cost(0, MIB),
        name="pick",
    )(local[0, True], local[0, False], halo[0, True], halo[0, False])
    if one_swap:
        sides = [lax.ppermute(picked[0], "col", [(0, 1), (1, 0)])]
    else:
        sides = [
            lax.ppermute(picked[0], "col", [(i, i + 1) for i in range(cols_n - 1)]),
            lax.ppermute(picked[1], "col", [(i + 1, i) for i in range(cols_n - 1)]),
        ]

    taps = w_dilated.reshape(9 * br, br)
    rest = height - RR
    n_groups = len(groups)
    pick = lambda table, near: [table[i, near] for i in range(n_groups)]
    flops = 2 * width * 3 * br * br
    out, partial = pl.pallas_call(
        functools.partial(conv_early, groups, cols_n, height),
        out_shape=[
            jax.ShapeDtypeStruct((height, width, br), BF16),
            jax.ShapeDtypeStruct((RR * width, br), F32),
        ],
        in_specs=[VM] * (1 + 3 * n_groups + len(sides)),
        out_specs=[HBM, VM],
        scratch_shapes=[
            pltpu.VMEM((height + RR, width + 2 * TILE, br), BF16),
            pltpu.VMEM((height + RR, width, 3 * br), BF16),
            pltpu.VMEM((rest, width, br), BF16),
            pltpu.SemaphoreType.DMA,
        ],
        compiler_params=params(CONV_MIB),
        cost_estimate=cost(flops * (3 * rest + 2 * RR), 4 * MIB),
        name="conv_early",
    )(taps, *pick(local, True), *pick(local, False), *pick(halo, True), *sides)
    n_in = 2 + n_groups + len(sides)
    return pl.pallas_call(
        functools.partial(conv_late, groups, cols_n, height),
        out_shape=jax.ShapeDtypeStruct((height, width, br), BF16),
        in_specs=[VM] * n_in + [HBM],
        out_specs=HBM,
        input_output_aliases={n_in: 0},
        scratch_shapes=[
            pltpu.VMEM((RR, width + 2 * TILE, br), BF16),
            pltpu.VMEM((RR, width, 3 * br), BF16),
            pltpu.VMEM((RR, width, br), BF16),
            pltpu.SemaphoreType.DMA((LATE,)),
        ],
        compiler_params=params(16),
        cost_estimate=cost(flops * RR, 2 * MIB),
        name="conv_late",
    )(taps, partial, *pick(halo, False), *sides, out)


def solution(mesh):
    in_specs = (
        P(("groups", "row"), "col", None, None),
        P(("groups", "row"), "col"),
        P(),
        P(),
        P(),
        P(),
        P(),
    )
    out_specs = P(("groups", "row"), "col", None)

    return jax.shard_map(shards, mesh=mesh, in_specs=in_specs, out_specs=out_specs, check_vma=False)
```

```python
import functools

import jax
import jax.numpy as jnp
from jax import lax
from jax.experimental import pallas as pl
from jax.experimental.pallas import tpu as pltpu
from jax.sharding import PartitionSpec as P


TILE = 16
RR = 18
RC = 15
BLOCK = 512
DEPTH = 3
F32 = jnp.float32
BF16 = jnp.bfloat16
VM = pl.BlockSpec(memory_space=pltpu.VMEM)
SM = pl.BlockSpec(memory_space=pltpu.SMEM)
HBM = pl.BlockSpec(memory_space=pltpu.MemorySpace.HBM)
MIB = 1 << 20
TRUNK_MIB = 16
CONV_MIB = 24


def params(mib):
    return pltpu.CompilerParams(vmem_limit_bytes=mib * MIB)


def cost(flops, nbytes):
    return pl.CostEstimate(flops=int(flops), bytes_accessed=int(nbytes), transcendentals=0)


def in_hbm(value):
    return pltpu.with_memory_space_constraint(value, pltpu.MemorySpace.HBM)


def near_is_top():
    return lax.rem(lax.axis_index("row"), 2)


def top_of(near_first):
    return near_is_top() if near_first else 1 - near_is_top()


def columns_of(chunk):
    return chunk[0]


def span(chunk, height):
    return (RR if chunk[1] else height - RR) * TILE


def sources(chunk, top):
    rest = (RR - TILE) * TILE
    pixels = TILE * TILE
    for j, col in enumerate(chunk[0]):
        if chunk[1]:
            at = j * (pixels + rest)
            yield 1 - top, col, 0, pixels, at
            yield top, col, (1 - top) * (pixels - rest), rest, at + pixels
        else:
            yield top, col, top * rest, pixels - rest, j * (pixels - rest)


def trunk_rows(x, wr, we, ws, wb, ready=lambda k: None):
    ready(0)
    hidden = jnp.maximum(jnp.dot(x, wr[...], preferred_element_type=F32), 0).astype(BF16)
    total = None
    for k, at in enumerate(range(0, we.shape[1], BLOCK)):
        ready(1 + k)
        summed = jnp.dot(hidden, we[:, at : at + BLOCK], preferred_element_type=F32)
        summed = summed + jnp.dot(x, ws[:, at : at + BLOCK], preferred_element_type=F32)
        block_out = jnp.maximum(summed, 0).astype(BF16)
        term = jnp.dot(block_out, wb[at : at + BLOCK, :], preferred_element_type=F32)
        total = term if total is None else total + term
    return jnp.maximum(total, 0)


def put_column(part, chunk, col, j, top, flags, out):
    width = part.shape[-1]
    where = pl.ds(j * TILE, TILE)
    own = flags[top, col] >= 0
    if chunk[1]:
        pixels = TILE * TILE
        full = jnp.where(flags[1 - top, col] >= 0, part[:pixels], 0.0).astype(BF16)
        rest = jnp.where(own, part[pixels:], 0.0).astype(BF16)
        out[pl.ds((1 - top) * (RR - TILE), TILE), where, :] = full.reshape(TILE, TILE, width)
        out[pl.ds(top * TILE, RR - TILE), where, :] = rest.reshape(RR - TILE, TILE, width)
    else:
        rows = part.shape[0] // TILE
        part = jnp.where(own, part, 0.0).astype(BF16)
        out[pl.ds(top * (RR - rows), rows), where, :] = part.reshape(rows, TILE, width)


def first_chunk(chunks, height, asg, feats, wr_h, we_h, ws_h, wb_h, out, xs, wr, we, ws, wb, flags, sems):
    steps = [[]]
    steps[0].append((asg, flags))
    at = 0
    later = []
    for i, chunk in enumerate(chunks):
        moves = [
            (feats.at[tr, col, pl.ds(first, count), :], xs.at[pl.ds(at + row, count), :])
            for tr, col, first, count, row in sources(chunk, top_of(chunk[2]))
        ]
        at += span(chunk, height) * len(columns_of(chunk))
        if i == 0:
            steps[0] += moves
        else:
            later += moves
    steps[0].append((wr_h, wr))
    for k in range(0, we.shape[1], BLOCK):
        cols = pl.ds(k, BLOCK)
        steps.append(
            [(ws_h.at[:, cols], ws.at[:, cols]), (we_h.at[:, cols], we.at[:, cols]), (wb_h.at[cols, :], wb.at[cols, :])]
        )
    n_weights = len(steps)
    steps.append(later)
    copies = []
    used = 0
    for step in steps:
        copies.append([pltpu.make_async_copy(src, dst, sems.at[used + j]) for j, (src, dst) in enumerate(step)])
        used += len(step)

    def begin(k):
        if k < len(copies):
            for copy in copies[k]:
                copy.start()

    def ready(k):
        for copy in copies[k]:
            copy.wait()
        begin(k + DEPTH)

    for k in range(DEPTH):
        begin(k)
    ready(0)
    per = span(chunks[0], height)
    cols = columns_of(chunks[0])
    reduced = trunk_rows(xs[0 : per * len(cols), :], wr, we, ws, wb, lambda k: ready(k) if k else None)
    for j, col in enumerate(cols):
        put_column(reduced[j * per : (j + 1) * per], chunks[0], col, j, top_of(chunks[0][2]), flags, out)
    for k in range(n_weights, len(copies)):
        ready(k)


def later_chunk(chunk, at, height, flags, xs, wr, we, ws, wb, *refs):
    out = refs[-1]
    top = top_of(chunk[2])
    per = span(chunk, height)
    cols = columns_of(chunk)

    def busy(col):
        own = flags[top, col] >= 0
        if chunk[1]:
            own = own | (flags[1 - top, col] >= 0)
        return own

    active = [busy(col) for col in cols]
    every = functools.reduce(lambda a, b: a & b, active)
    zero = jnp.zeros((span(chunk, height), out.shape[-1]), F32)

    @pl.when(every)
    def _():
        reduced = trunk_rows(xs[at : at + per * len(cols), :], wr, we, ws, wb)
        for j, col in enumerate(cols):
            put_column(reduced[j * per : (j + 1) * per], chunk, col, j, top, flags, out)

    if len(cols) == 1:
        @pl.when(jnp.logical_not(every))
        def _():
            put_column(zero, chunk, cols[0], 0, top, flags, out)
    else:
        for j, col in enumerate(cols):
            @pl.when(jnp.logical_not(active[j]))
            def _():
                put_column(zero, chunk, col, j, top, flags, out)

        one = cols[0]
        step = cols[1] - cols[0]

        @pl.loop(0, len(cols))
        def _(j):
            col = one + j * step
            mine = flags[top, col] >= 0
            if chunk[1]:
                mine = mine | (flags[1 - top, col] >= 0)

            @pl.when(mine & jnp.logical_not(every))
            def _():
                rows = pl.ds(pl.multiple_of(at + j * per, TILE), per)
                put_column(trunk_rows(xs[rows, :], wr, we, ws, wb), chunk, col, j, top, flags, out)

    if not chunk[1]:
        near = refs[0]
        shared = 2 * RR - height
        out[pl.ds((1 - top) * (RR - shared), shared)] = near[pl.ds(top * (RR - shared), shared)]


def pick_kernel(cols_n, *refs):
    n = 1 if cols_n == 2 else 2
    ins, outs = refs[:-n], refs[-n:]
    width = ins[0].shape[1]
    for i, src in enumerate(ins):
        rows = pl.ds(i * RR, RR)
        if cols_n == 2:
            first = pl.multiple_of((1 - lax.axis_index("col")) * (width - TILE), TILE)
            outs[0][rows] = src[:, pl.ds(first, TILE), :]
        else:
            outs[0][rows] = src[:, width - TILE :, :]
            outs[1][rows] = src[:, :TILE, :]


def place(cols, src, first, count, ext, row):
    for j, col in enumerate(cols):
        ext[pl.ds(row, count), (1 + col) * TILE : (2 + col) * TILE, :] = src[
            pl.ds(first, count), j * TILE : (j + 1) * TILE, :
        ]


def place_sides(cols_n, sides, part, first, count, ext, row):
    me = lax.axis_index("col")
    wide = ext.shape[1]
    for on, at, ref in ((me > 0, 0, sides[0]), (me < cols_n - 1, wide - TILE, sides[-1])):
        there = ref[pl.ds(part * RR + first, count)]
        ext[pl.ds(row, count), at : at + TILE, :] = jnp.where(on, there, jnp.zeros_like(there))


def spread(ext, cat, width):
    br = ext.shape[-1]
    for b in range(3):
        left = TILE - RC + b * RC
        cat[:, :, b * br : (b + 1) * br] = ext[:, left : left + width, :]


def conv_early(groups, cols_n, height, w, *refs):
    g = len(groups)
    ones, twos = refs[:g], refs[g : 2 * g]
    sides = refs[2 * g : -3]
    partial, ext, cat = refs[-3:]
    width = cat.shape[1]
    rest = height - RR
    for i, (cols, near_first) in enumerate(groups):
        up = top_of(near_first)
        skip = up * (RR - rest)
        for part, src, first, count, row in ((0, ones[i], 0, RR, (1 - up) * rest), (1, twos[i], skip, rest, up * RR)):
            place(cols, src, first, count, ext, row)
            if i == 0:
                place_sides(cols_n, sides, part, first, count, ext, row)
    spread(ext, cat, width)
    k = cat.shape[2]
    for at, count in blocks_of(height):
        total = None
        for a in range(3):
            row = at + (a - 1) * RR
            if 0 <= row < height:
                taps = cat[row : row + count].reshape(count * width, k)
                term = jnp.dot(taps, w[a * k : (a + 1) * k, :], preferred_element_type=F32)
                total = term if total is None else total + term
        partial[at * width : (at + count) * width, :] = total


def conv_late(groups, cols_n, height, w, partial, *refs):
    g = len(groups)
    near, far = refs[:g], refs[g : 2 * g]
    sides = refs[2 * g : -5]
    out, ext, cat, done, sems = refs[-5:]
    top = near_is_top()
    width = cat.shape[1]
    for part, halo, row in ((2, near, (1 - top) * RR), (3, far, top * RR)):
        for i, (cols, _) in enumerate(groups):
            place(cols, halo[i], 0, RR, ext, row)
        place_sides(cols_n, sides, part, 0, RR, ext, row)
    spread(ext, cat, width)
    k = cat.shape[2]
    copies = []
    for n, (at, count) in enumerate(blocks_of(height)):
        total = partial[at * width : (at + count) * width, :]
        for a, row in ((0, at if at < RR else -1), (2, at - height + 2 * RR if at >= height - RR else -1)):
            if row >= 0:
                taps = cat[row : row + count].reshape(count * width, k)
                total = total + jnp.dot(taps, w[a * k : (a + 1) * k, :], preferred_element_type=F32)
        done[at : at + count] = jnp.maximum(total, 0).astype(BF16).reshape(count, width, done.shape[2])
        copies.append(pltpu.make_async_copy(done.at[pl.ds(at, count)], out.at[pl.ds(at, count)], sems.at[n]))
        copies[-1].start()
    for copy in copies:
        copy.wait()


def blocks_of(height):
    rest = height - RR
    cuts = [0, rest // 2, rest, RR, RR + rest // 2, height]
    return [(lo, hi - lo) for lo, hi in zip(cuts, cuts[1:]) if hi > lo]


def plan(tile_cols):
    groups = [([0, tile_cols - 1], True), (list(range(1, tile_cols - 1)), True)]
    order = [(0, True), (0, False), (1, True), (1, False)]
    return groups, order


def shards(features, assignment, w_reduce, w_expand, w_short, w_branch, w_dilated):
    tile_rows, tile_cols, pixels, channels = features.shape
    mid, cout, br = w_reduce.shape[1], w_expand.shape[1], w_branch.shape[1]
    height, width = tile_rows * TILE, tile_cols * TILE
    assert tile_rows == 2 and pixels == TILE * TILE and TILE < RR <= height <= 2 * RR
    groups, order = plan(tile_cols)
    chunks = [(groups[i][0], one, groups[i][1]) for i, one in order]
    sizes = [span(c, height) * len(c[0]) for c in chunks]
    starts = [sum(sizes[:i]) for i in range(len(sizes))]
    per_row = 2 * (channels * mid + mid * cout + channels * cout + cout * br)
    n_copies = sum(len(list(sources(c, 0))) for c in chunks) + 2 + 3 * (cout // BLOCK)

    def grid_of(cols):
        return jax.ShapeDtypeStruct((RR, len(cols) * TILE, br), BF16)

    first, xs, wr, we, ws, wb = pl.pallas_call(
        functools.partial(first_chunk, chunks, height),
        out_shape=[
            grid_of(chunks[0][0]),
            jax.ShapeDtypeStruct((sum(sizes), channels), BF16),
            jax.ShapeDtypeStruct(w_reduce.shape, BF16),
            jax.ShapeDtypeStruct(w_expand.shape, BF16),
            jax.ShapeDtypeStruct(w_short.shape, BF16),
            jax.ShapeDtypeStruct(w_branch.shape, BF16),
        ],
        in_specs=[HBM] * 6,
        out_specs=[VM] * 6,
        scratch_shapes=[pltpu.SMEM(assignment.shape, jnp.int32), pltpu.SemaphoreType.DMA((n_copies,))],
        compiler_params=params(TRUNK_MIB),
        cost_estimate=cost(per_row * sizes[0], 12 * MIB),
        name="trunk_first",
    )(*[in_hbm(v) for v in (assignment, features, w_reduce, w_expand, w_short, w_branch)])

    rows_n = lax.axis_size("row")
    swap = [(i, i ^ 1) for i in range(rows_n) if i ^ 1 < rows_n]
    cross = [pair for i in range(1, rows_n - 1, 2) for pair in ((i, i + 1), (i + 1, i))]

    local, halo = {}, {}
    for n, (i, one) in enumerate(order):
        if n == 0:
            value = first
        else:
            extra = [] if one else [local[i, True]]
            value = pl.pallas_call(
                functools.partial(later_chunk, chunks[n], starts[n], height),
                out_shape=grid_of(groups[i][0]),
                in_specs=[SM] + [VM] * (5 + len(extra)),
                out_specs=VM,
                compiler_params=params(TRUNK_MIB),
                cost_estimate=cost(per_row * sizes[n], MIB),
            )(assignment, xs, wr, we, ws, wb, *extra)
        local[i, one] = value
        near = one == groups[i][1]
        halo[i, near] = lax.ppermute(value, "row", swap if near else cross)

    cols_n = lax.axis_size("col")
    side = jax.ShapeDtypeStruct((4 * RR, TILE, br), BF16)
    one_swap = cols_n == 2
    picked = pl.pallas_call(
        functools.partial(pick_kernel, cols_n),
        out_shape=[side] if one_swap else [side, side],
        in_specs=[VM] * 4,
        out_specs=[VM] * (1 if one_swap else 2),
        compiler_params=params(4),
        cost_estimate=cost(0, MIB),
        name="pick",
    )(local[0, True], local[0, False], halo[0, True], halo[0, False])
    if one_swap:
        sides = [lax.ppermute(picked[0], "col", [(0, 1), (1, 0)])]
    else:
        sides = [
            lax.ppermute(picked[0], "col", [(i, i + 1) for i in range(cols_n - 1)]),
            lax.ppermute(picked[1], "col", [(i + 1, i) for i in range(cols_n - 1)]),
        ]

    taps = w_dilated.reshape(9 * br, br)
    n_groups = len(groups)
    pick = lambda table, key: [table[i, key] for i in range(n_groups)]
    flops = 2 * width * 3 * br * br
    partial = pl.pallas_call(
        functools.partial(conv_early, groups, cols_n, height),
        out_shape=jax.ShapeDtypeStruct((height * width, br), F32),
        in_specs=[VM] * (1 + 2 * n_groups + len(sides)),
        out_specs=VM,
        scratch_shapes=[pltpu.VMEM((height, width + 2 * TILE, br), BF16), pltpu.VMEM((height, width, 3 * br), BF16)],
        compiler_params=params(CONV_MIB),
        cost_estimate=cost(flops * (3 * height - 2 * RR), 4 * MIB),
        name="conv_early",
    )(taps, *pick(local, True), *pick(local, False), *sides)
    return pl.pallas_call(
        functools.partial(conv_late, groups, cols_n, height),
        out_shape=jax.ShapeDtypeStruct((height, width, br), BF16),
        in_specs=[VM] * (2 + 2 * n_groups + len(sides)),
        out_specs=HBM,
        scratch_shapes=[
            pltpu.VMEM((2 * RR, width + 2 * TILE, br), BF16),
            pltpu.VMEM((2 * RR, width, 3 * br), BF16),
            pltpu.VMEM((height, width, br), BF16),
            pltpu.SemaphoreType.DMA((len(blocks_of(height)),)),
        ],
        compiler_params=params(CONV_MIB),
        cost_estimate=cost(flops * 2 * RR, 4 * MIB),
        name="conv_late",
    )(taps, partial, *pick(halo, True), *pick(halo, False), *sides)


def solution(mesh):
    in_specs = (
        P(("groups", "row"), "col", None, None),
        P(("groups", "row"), "col"),
        P(),
        P(),
        P(),
        P(),
        P(),
    )
    out_specs = P(("groups", "row"), "col", None)

    return jax.shard_map(shards, mesh=mesh, in_specs=in_specs, out_specs=out_specs, check_vma=False)
```

```python
import functools

import jax
import jax.numpy as jnp
from jax import lax
from jax.experimental import pallas as pl
from jax.experimental.pallas import tpu as pltpu
from jax.sharding import PartitionSpec as P


TILE = 16
RR = 18
RC = 15
BLOCK = 512
DEPTH = 3
F32 = jnp.float32
BF16 = jnp.bfloat16
VM = pl.BlockSpec(memory_space=pltpu.VMEM)
SM = pl.BlockSpec(memory_space=pltpu.SMEM)
HBM = pl.BlockSpec(memory_space=pltpu.MemorySpace.HBM)
MIB = 1 << 20
TRUNK_MIB = 16
CONV_MIB = 24


def params(mib):
    return pltpu.CompilerParams(vmem_limit_bytes=mib * MIB)


def cost(flops, nbytes):
    return pl.CostEstimate(flops=int(flops), bytes_accessed=int(nbytes), transcendentals=0)


def in_hbm(value):
    return pltpu.with_memory_space_constraint(value, pltpu.MemorySpace.HBM)


def near_is_top():
    return lax.rem(lax.axis_index("row"), 2)


def top_of(near_first):
    return near_is_top() if near_first else 1 - near_is_top()


def columns_of(chunk):
    return chunk[0]


def span(chunk, height):
    return (RR if chunk[1] else height - RR) * TILE


def sources(chunk, top):
    rest = (RR - TILE) * TILE
    pixels = TILE * TILE
    for j, col in enumerate(chunk[0]):
        if chunk[1]:
            at = j * (pixels + rest)
            yield 1 - top, col, 0, pixels, at
            yield top, col, (1 - top) * (pixels - rest), rest, at + pixels
        else:
            yield top, col, top * rest, pixels - rest, j * (pixels - rest)


def trunk_rows(x, wr, we, ws, wb, ready=lambda k: None):
    ready(0)
    hidden = jnp.maximum(jnp.dot(x, wr[...], preferred_element_type=F32), 0).astype(BF16)
    total = None
    for k, at in enumerate(range(0, we.shape[1], BLOCK)):
        ready(1 + k)
        summed = jnp.dot(hidden, we[:, at : at + BLOCK], preferred_element_type=F32)
        summed = summed + jnp.dot(x, ws[:, at : at + BLOCK], preferred_element_type=F32)
        block_out = jnp.maximum(summed, 0).astype(BF16)
        term = jnp.dot(block_out, wb[at : at + BLOCK, :], preferred_element_type=F32)
        total = term if total is None else total + term
    return jnp.maximum(total, 0)


def put_column(part, chunk, col, j, top, flags, out):
    width = part.shape[-1]
    where = pl.ds(j * TILE, TILE)
    own = flags[top, col] >= 0
    if chunk[1]:
        pixels = TILE * TILE
        full = jnp.where(flags[1 - top, col] >= 0, part[:pixels], 0.0).astype(BF16)
        rest = jnp.where(own, part[pixels:], 0.0).astype(BF16)
        out[pl.ds((1 - top) * (RR - TILE), TILE), where, :] = full.reshape(TILE, TILE, width)
        out[pl.ds(top * TILE, RR - TILE), where, :] = rest.reshape(RR - TILE, TILE, width)
    else:
        rows = part.shape[0] // TILE
        part = jnp.where(own, part, 0.0).astype(BF16)
        out[pl.ds(top * (RR - rows), rows), where, :] = part.reshape(rows, TILE, width)


def first_chunk(chunks, height, asg, feats, wr_h, we_h, ws_h, wb_h, out, xs, wr, we, ws, wb, flags, sems):
    steps = [[]]
    steps[0].append((asg, flags))
    at = 0
    later = []
    for i, chunk in enumerate(chunks):
        moves = [
            (feats.at[tr, col, pl.ds(first, count), :], xs.at[pl.ds(at + row, count), :])
            for tr, col, first, count, row in sources(chunk, top_of(chunk[2]))
        ]
        at += span(chunk, height) * len(columns_of(chunk))
        if i == 0:
            steps[0] += moves
        else:
            later += moves
    steps[0].append((wr_h, wr))
    for k in range(0, we.shape[1], BLOCK):
        cols = pl.ds(k, BLOCK)
        steps.append(
            [(ws_h.at[:, cols], ws.at[:, cols]), (we_h.at[:, cols], we.at[:, cols]), (wb_h.at[cols, :], wb.at[cols, :])]
        )
    n_weights = len(steps)
    steps.append(later)
    copies = []
    used = 0
    for step in steps:
        copies.append([pltpu.make_async_copy(src, dst, sems.at[used + j]) for j, (src, dst) in enumerate(step)])
        used += len(step)

    def begin(k):
        if k < len(copies):
            for copy in copies[k]:
                copy.start()

    def ready(k):
        for copy in copies[k]:
            copy.wait()
        begin(k + DEPTH)

    for k in range(DEPTH):
        begin(k)
    ready(0)
    per = span(chunks[0], height)
    cols = columns_of(chunks[0])
    reduced = trunk_rows(xs[0 : per * len(cols), :], wr, we, ws, wb, lambda k: ready(k) if k else None)
    for j, col in enumerate(cols):
        put_column(reduced[j * per : (j + 1) * per], chunks[0], col, j, top_of(chunks[0][2]), flags, out)
    for k in range(n_weights, len(copies)):
        ready(k)


def later_chunk(chunk, at, height, flags, xs, wr, we, ws, wb, *refs):
    out = refs[-1]
    top = top_of(chunk[2])
    per = span(chunk, height)
    cols = columns_of(chunk)

    def busy(col):
        own = flags[top, col] >= 0
        if chunk[1]:
            own = own | (flags[1 - top, col] >= 0)
        return own

    active = [busy(col) for col in cols]
    every = functools.reduce(lambda a, b: a & b, active)
    zero = jnp.zeros((span(chunk, height), out.shape[-1]), F32)

    @pl.when(every)
    def _():
        reduced = trunk_rows(xs[at : at + per * len(cols), :], wr, we, ws, wb)
        for j, col in enumerate(cols):
            put_column(reduced[j * per : (j + 1) * per], chunk, col, j, top, flags, out)

    if len(cols) == 1:
        @pl.when(jnp.logical_not(every))
        def _():
            put_column(zero, chunk, cols[0], 0, top, flags, out)
    else:
        for j, col in enumerate(cols):
            @pl.when(jnp.logical_not(active[j]))
            def _():
                put_column(zero, chunk, col, j, top, flags, out)

        one = cols[0]
        step = cols[1] - cols[0]

        @pl.loop(0, len(cols))
        def _(j):
            col = one + j * step
            mine = flags[top, col] >= 0
            if chunk[1]:
                mine = mine | (flags[1 - top, col] >= 0)

            @pl.when(mine & jnp.logical_not(every))
            def _():
                rows = pl.ds(pl.multiple_of(at + j * per, TILE), per)
                put_column(trunk_rows(xs[rows, :], wr, we, ws, wb), chunk, col, j, top, flags, out)

    if not chunk[1]:
        near = refs[0]
        shared = 2 * RR - height
        out[pl.ds((1 - top) * (RR - shared), shared)] = near[pl.ds(top * (RR - shared), shared)]


def pick_kernel(cols_n, *refs):
    n = 1 if cols_n == 2 else 2
    ins, outs = refs[:-n], refs[-n:]
    width = ins[0].shape[1]
    for i, src in enumerate(ins):
        rows = pl.ds(i * RR, RR)
        if cols_n == 2:
            first = pl.multiple_of((1 - lax.axis_index("col")) * (width - TILE), TILE)
            outs[0][rows] = src[:, pl.ds(first, TILE), :]
        else:
            outs[0][rows] = src[:, width - TILE :, :]
            outs[1][rows] = src[:, :TILE, :]


def place(cols, src, first, count, ext, row, on=None):
    for j, col in enumerate(cols):
        there = src[pl.ds(first, count), j * TILE : (j + 1) * TILE, :]
        if on is not None:
            there = jnp.where(on, there, jnp.zeros_like(there))
        ext[pl.ds(row, count), (1 + col) * TILE : (2 + col) * TILE, :] = there


def place_sides(cols_n, sides, part, first, count, ext, row, on=None):
    me = lax.axis_index("col")
    wide = ext.shape[1]
    for here, at, ref in ((me > 0, 0, sides[0]), (me < cols_n - 1, wide - TILE, sides[-1])):
        there = ref[pl.ds(part * RR + first, count)]
        here = here if on is None else here & on
        ext[pl.ds(row, count), at : at + TILE, :] = jnp.where(here, there, jnp.zeros_like(there))


def spread(ext, cat, width):
    br = ext.shape[-1]
    for b in range(3):
        left = TILE - RC + b * RC
        cat[:, :, b * br : (b + 1) * br] = ext[:, left : left + width, :]


def conv_early(groups, cols_n, height, w, *refs):
    g = len(groups)
    ones, twos = refs[:g], refs[g : 2 * g]
    sides = refs[2 * g : -3]
    partial, ext, cat = refs[-3:]
    width = cat.shape[1]
    rest = height - RR
    for i, (cols, near_first) in enumerate(groups):
        up = top_of(near_first)
        skip = up * (RR - rest)
        for part, src, first, count, row in ((0, ones[i], 0, RR, (1 - up) * rest), (1, twos[i], skip, rest, up * RR)):
            place(cols, src, first, count, ext, row)
            if i == 0:
                place_sides(cols_n, sides, part, first, count, ext, row)
    spread(ext, cat, width)
    k = cat.shape[2]
    for at, count in blocks_of(height):
        total = None
        for a in range(3):
            row = at + (a - 1) * RR
            if 0 <= row < height:
                taps = cat[row : row + count].reshape(count * width, k)
                term = jnp.dot(taps, w[a * k : (a + 1) * k, :], preferred_element_type=F32)
                total = term if total is None else total + term
        partial[at * width : (at + count) * width, :] = total


def conv_late(groups, rows_n, cols_n, height, w, partial, *refs):
    g = len(groups)
    near, far = refs[:g], refs[g : 2 * g]
    sides = refs[2 * g : -5]
    out, ext, cat, done, sems = refs[-5:]
    top = near_is_top()
    width = cat.shape[1]
    me = lax.axis_index("row")
    inside = (me > 0) & (me < rows_n - 1)
    for part, halo, row, on in ((2, near, (1 - top) * RR, None), (3, far, top * RR, inside)):
        for i, (cols, _) in enumerate(groups):
            place(cols, halo[i], 0, RR, ext, row, on)
        place_sides(cols_n, sides, part, 0, RR, ext, row, on)
    spread(ext, cat, width)
    k = cat.shape[2]
    copies = []
    for n, (at, count) in enumerate(blocks_of(height)):
        total = partial[at * width : (at + count) * width, :]
        for a, row in ((0, at if at < RR else -1), (2, at - height + 2 * RR if at >= height - RR else -1)):
            if row >= 0:
                taps = cat[row : row + count].reshape(count * width, k)
                total = total + jnp.dot(taps, w[a * k : (a + 1) * k, :], preferred_element_type=F32)
        done[at : at + count] = jnp.maximum(total, 0).astype(BF16).reshape(count, width, done.shape[2])
        copies.append(pltpu.make_async_copy(done.at[pl.ds(at, count)], out.at[pl.ds(at, count)], sems.at[n]))
        copies[-1].start()
    for copy in copies:
        copy.wait()


def blocks_of(height):
    rest = height - RR
    cuts = [0, rest // 2, rest, RR, RR + rest // 2, height]
    return [(lo, hi - lo) for lo, hi in zip(cuts, cuts[1:]) if hi > lo]


def plan(tile_cols):
    groups = [([0, tile_cols - 1], True), (list(range(1, tile_cols - 1)), True)]
    order = [(0, True), (0, False), (1, True), (1, False)]
    return groups, order


def shards(features, assignment, w_reduce, w_expand, w_short, w_branch, w_dilated):
    tile_rows, tile_cols, pixels, channels = features.shape
    mid, cout, br = w_reduce.shape[1], w_expand.shape[1], w_branch.shape[1]
    height, width = tile_rows * TILE, tile_cols * TILE
    assert tile_rows == 2 and pixels == TILE * TILE and TILE < RR <= height <= 2 * RR
    groups, order = plan(tile_cols)
    chunks = [(groups[i][0], one, groups[i][1]) for i, one in order]
    sizes = [span(c, height) * len(c[0]) for c in chunks]
    starts = [sum(sizes[:i]) for i in range(len(sizes))]
    per_row = 2 * (channels * mid + mid * cout + channels * cout + cout * br)
    n_copies = sum(len(list(sources(c, 0))) for c in chunks) + 2 + 3 * (cout // BLOCK)

    def grid_of(cols):
        return jax.ShapeDtypeStruct((RR, len(cols) * TILE, br), BF16)

    first, xs, wr, we, ws, wb = pl.pallas_call(
        functools.partial(first_chunk, chunks, height),
        out_shape=[
            grid_of(chunks[0][0]),
            jax.ShapeDtypeStruct((sum(sizes), channels), BF16),
            jax.ShapeDtypeStruct(w_reduce.shape, BF16),
            jax.ShapeDtypeStruct(w_expand.shape, BF16),
            jax.ShapeDtypeStruct(w_short.shape, BF16),
            jax.ShapeDtypeStruct(w_branch.shape, BF16),
        ],
        in_specs=[HBM] * 6,
        out_specs=[VM] * 6,
        scratch_shapes=[pltpu.SMEM(assignment.shape, jnp.int32), pltpu.SemaphoreType.DMA((n_copies,))],
        compiler_params=params(TRUNK_MIB),
        cost_estimate=cost(per_row * sizes[0], 12 * MIB),
        name="trunk_first",
    )(*[in_hbm(v) for v in (assignment, features, w_reduce, w_expand, w_short, w_branch)])

    rows_n, cols_n = lax.axis_size("row"), lax.axis_size("col")
    assert rows_n % 2 == 0 and cols_n % 2 == 0

    def partner(row, col, near):
        if near:
            return row ^ 1, col
        if row in (0, rows_n - 1):
            return row, col ^ 1
        return (row + 1 if row % 2 else row - 1), col

    def swap(near):
        pairs = []
        for row in range(rows_n):
            for col in range(cols_n):
                to_row, to_col = partner(row, col, near)
                pairs.append((row * cols_n + col, to_row * cols_n + to_col))
        return pairs

    local, halo = {}, {}
    for n, (i, one) in enumerate(order):
        if n == 0:
            value = first
        else:
            extra = [] if one else [local[i, True]]
            value = pl.pallas_call(
                functools.partial(later_chunk, chunks[n], starts[n], height),
                out_shape=grid_of(groups[i][0]),
                in_specs=[SM] + [VM] * (5 + len(extra)),
                out_specs=VM,
                compiler_params=params(TRUNK_MIB),
                cost_estimate=cost(per_row * sizes[n], MIB),
            )(assignment, xs, wr, we, ws, wb, *extra)
        local[i, one] = value
        near = one == groups[i][1]
        halo[i, near] = lax.ppermute(value, ("row", "col"), swap(near))

    side = jax.ShapeDtypeStruct((4 * RR, TILE, br), BF16)
    one_swap = cols_n == 2
    picked = pl.pallas_call(
        functools.partial(pick_kernel, cols_n),
        out_shape=[side] if one_swap else [side, side],
        in_specs=[VM] * 4,
        out_specs=[VM] * (1 if one_swap else 2),
        compiler_params=params(4),
        cost_estimate=cost(0, MIB),
        name="pick",
    )(local[0, True], local[0, False], halo[0, True], halo[0, False])
    if one_swap:
        sides = [lax.ppermute(picked[0], "col", [(0, 1), (1, 0)])]
    else:
        sides = [
            lax.ppermute(picked[0], "col", [(i, i + 1) for i in range(cols_n - 1)]),
            lax.ppermute(picked[1], "col", [(i + 1, i) for i in range(cols_n - 1)]),
        ]

    taps = w_dilated.reshape(9 * br, br)
    n_groups = len(groups)
    pick = lambda table, key: [table[i, key] for i in range(n_groups)]
    flops = 2 * width * 3 * br * br
    partial = pl.pallas_call(
        functools.partial(conv_early, groups, cols_n, height),
        out_shape=jax.ShapeDtypeStruct((height * width, br), F32),
        in_specs=[VM] * (1 + 2 * n_groups + len(sides)),
        out_specs=VM,
        scratch_shapes=[pltpu.VMEM((height, width + 2 * TILE, br), BF16), pltpu.VMEM((height, width, 3 * br), BF16)],
        compiler_params=params(CONV_MIB),
        cost_estimate=cost(flops * (3 * height - 2 * RR), 4 * MIB),
        name="conv_early",
    )(taps, *pick(local, True), *pick(local, False), *sides)
    return pl.pallas_call(
        functools.partial(conv_late, groups, rows_n, cols_n, height),
        out_shape=jax.ShapeDtypeStruct((height, width, br), BF16),
        in_specs=[VM] * (2 + 2 * n_groups + len(sides)),
        out_specs=HBM,
        scratch_shapes=[
            pltpu.VMEM((2 * RR, width + 2 * TILE, br), BF16),
            pltpu.VMEM((2 * RR, width, 3 * br), BF16),
            pltpu.VMEM((height, width, br), BF16),
            pltpu.SemaphoreType.DMA((len(blocks_of(height)),)),
        ],
        compiler_params=params(CONV_MIB),
        cost_estimate=cost(flops * 2 * RR, 4 * MIB),
        name="conv_late",
    )(taps, partial, *pick(halo, True), *pick(halo, False), *sides)


def solution(mesh):
    in_specs = (
        P(("groups", "row"), "col", None, None),
        P(("groups", "row"), "col"),
        P(),
        P(),
        P(),
        P(),
        P(),
    )
    out_specs = P(("groups", "row"), "col", None)

    return jax.shard_map(shards, mesh=mesh, in_specs=in_specs, out_specs=out_specs, check_vma=False)
```

```python
import functools

import jax
import jax.numpy as jnp
from jax import lax
from jax.experimental import pallas as pl
from jax.experimental.pallas import tpu as pltpu
from jax.sharding import PartitionSpec as P


TILE = 16
RR = 18
RC = 15
BLOCK = 512
DEPTH = 3
WAITS = (1, 3)
F32 = jnp.float32
BF16 = jnp.bfloat16
VM = pl.BlockSpec(memory_space=pltpu.VMEM)
SM = pl.BlockSpec(memory_space=pltpu.SMEM)
HBM = pl.BlockSpec(memory_space=pltpu.MemorySpace.HBM)
MIB = 1 << 20
TRUNK_MIB = 16
CONV_MIB = 24


def params(mib):
    return pltpu.CompilerParams(vmem_limit_bytes=mib * MIB)


def cost(flops, nbytes):
    return pl.CostEstimate(flops=int(flops), bytes_accessed=int(nbytes), transcendentals=0)


def in_hbm(value):
    return pltpu.with_memory_space_constraint(value, pltpu.MemorySpace.HBM)


def near_is_top():
    return lax.rem(lax.axis_index("row"), 2)


def top_of(near_first):
    return near_is_top() if near_first else 1 - near_is_top()


def columns_of(chunk):
    return chunk[0]


def span(chunk, height):
    return (RR if chunk[1] else height - RR) * TILE


def sources(chunk, top):
    rest = (RR - TILE) * TILE
    pixels = TILE * TILE
    for j, col in enumerate(chunk[0]):
        if chunk[1]:
            at = j * (pixels + rest)
            yield 1 - top, col, 0, pixels, at
            yield top, col, (1 - top) * (pixels - rest), rest, at + pixels
        else:
            yield top, col, top * rest, pixels - rest, j * (pixels - rest)


def trunk_rows(x, wr, we, ws, wb, ready=lambda k: None):
    ready(0)
    hidden = jnp.maximum(jnp.dot(x, wr[...], preferred_element_type=F32), 0).astype(BF16)
    total = None
    for k, at in enumerate(range(0, we.shape[1], BLOCK)):
        ready(1 + k)
        summed = jnp.dot(hidden, we[:, at : at + BLOCK], preferred_element_type=F32)
        summed = summed + jnp.dot(x, ws[:, at : at + BLOCK], preferred_element_type=F32)
        block_out = jnp.maximum(summed, 0).astype(BF16)
        term = jnp.dot(block_out, wb[at : at + BLOCK, :], preferred_element_type=F32)
        total = term if total is None else total + term
    return jnp.maximum(total, 0)


def put_column(part, chunk, col, j, top, flags, out):
    width = part.shape[-1]
    where = pl.ds(j * TILE, TILE)
    own = flags[top, col] >= 0
    if chunk[1]:
        pixels = TILE * TILE
        full = jnp.where(flags[1 - top, col] >= 0, part[:pixels], 0.0).astype(BF16)
        rest = jnp.where(own, part[pixels:], 0.0).astype(BF16)
        out[pl.ds((1 - top) * (RR - TILE), TILE), where, :] = full.reshape(TILE, TILE, width)
        out[pl.ds(top * TILE, RR - TILE), where, :] = rest.reshape(RR - TILE, TILE, width)
    else:
        rows = part.shape[0] // TILE
        part = jnp.where(own, part, 0.0).astype(BF16)
        out[pl.ds(top * (RR - rows), rows), where, :] = part.reshape(rows, TILE, width)


def first_chunk(chunks, height, asg, feats, wr_h, we_h, ws_h, wb_h, out, xs, wr, we, ws, wb, flags, sems):
    steps = [[]]
    steps[0].append((asg, flags))
    at = 0
    later = []
    for i, chunk in enumerate(chunks):
        moves = [
            (feats.at[tr, col, pl.ds(first, count), :], xs.at[pl.ds(at + row, count), :])
            for tr, col, first, count, row in sources(chunk, top_of(chunk[2]))
        ]
        at += span(chunk, height) * len(columns_of(chunk))
        if i == 0:
            steps[0] += moves
        else:
            later += moves
    steps[0].append((wr_h, wr))
    ends = [sum(WAITS[: i + 1]) for i in range(len(WAITS))]
    first_of = {}
    for i, n_blocks in enumerate(WAITS):
        first_of[1 + ends[i] - n_blocks] = 1 + i
        cols = pl.ds((ends[i] - n_blocks) * BLOCK, n_blocks * BLOCK)
        steps.append(
            [(ws_h.at[:, cols], ws.at[:, cols]), (we_h.at[:, cols], we.at[:, cols]), (wb_h.at[cols, :], wb.at[cols, :])]
        )
    n_weights = len(steps)
    steps.append(later)
    copies = []
    used = 0
    for step in steps:
        copies.append([pltpu.make_async_copy(src, dst, sems.at[used + j]) for j, (src, dst) in enumerate(step)])
        used += len(step)

    def begin(k):
        if k < len(copies):
            for copy in copies[k]:
                copy.start()

    def ready(k):
        for copy in copies[k]:
            copy.wait()
        begin(k + DEPTH)

    for k in range(DEPTH):
        begin(k)
    ready(0)
    per = span(chunks[0], height)
    cols = columns_of(chunks[0])
    reduced = trunk_rows(xs[0 : per * len(cols), :], wr, we, ws, wb, lambda k: ready(first_of[k]) if k in first_of else None)
    for j, col in enumerate(cols):
        put_column(reduced[j * per : (j + 1) * per], chunks[0], col, j, top_of(chunks[0][2]), flags, out)
    for k in range(n_weights, len(copies)):
        ready(k)


def later_chunk(chunk, at, height, flags, xs, wr, we, ws, wb, *refs):
    out = refs[-1]
    top = top_of(chunk[2])
    per = span(chunk, height)
    cols = columns_of(chunk)

    def busy(col):
        own = flags[top, col] >= 0
        if chunk[1]:
            own = own | (flags[1 - top, col] >= 0)
        return own

    active = [busy(col) for col in cols]
    every = functools.reduce(lambda a, b: a & b, active)
    zero = jnp.zeros((span(chunk, height), out.shape[-1]), F32)

    @pl.when(every)
    def _():
        reduced = trunk_rows(xs[at : at + per * len(cols), :], wr, we, ws, wb)
        for j, col in enumerate(cols):
            put_column(reduced[j * per : (j + 1) * per], chunk, col, j, top, flags, out)

    if len(cols) == 1:
        @pl.when(jnp.logical_not(every))
        def _():
            put_column(zero, chunk, cols[0], 0, top, flags, out)
    else:
        for j, col in enumerate(cols):
            @pl.when(jnp.logical_not(active[j]))
            def _():
                put_column(zero, chunk, col, j, top, flags, out)

        one = cols[0]
        step = cols[1] - cols[0]

        @pl.loop(0, len(cols))
        def _(j):
            col = one + j * step
            mine = flags[top, col] >= 0
            if chunk[1]:
                mine = mine | (flags[1 - top, col] >= 0)

            @pl.when(mine & jnp.logical_not(every))
            def _():
                rows = pl.ds(pl.multiple_of(at + j * per, TILE), per)
                put_column(trunk_rows(xs[rows, :], wr, we, ws, wb), chunk, col, j, top, flags, out)

    if not chunk[1]:
        near = refs[0]
        shared = 2 * RR - height
        out[pl.ds((1 - top) * (RR - shared), shared)] = near[pl.ds(top * (RR - shared), shared)]


def pick_kernel(cols_n, *refs):
    n = 1 if cols_n == 2 else 2
    ins, outs = refs[:-n], refs[-n:]
    width = ins[0].shape[1]
    for i, src in enumerate(ins):
        rows = pl.ds(i * RR, RR)
        if cols_n == 2:
            first = pl.multiple_of((1 - lax.axis_index("col")) * (width - TILE), TILE)
            outs[0][rows] = src[:, pl.ds(first, TILE), :]
        else:
            outs[0][rows] = src[:, width - TILE :, :]
            outs[1][rows] = src[:, :TILE, :]


def place(cols, src, first, count, ext, row, on=None):
    for j, col in enumerate(cols):
        there = src[pl.ds(first, count), j * TILE : (j + 1) * TILE, :]
        if on is not None:
            there = jnp.where(on, there, jnp.zeros_like(there))
        ext[pl.ds(row, count), (1 + col) * TILE : (2 + col) * TILE, :] = there


def place_sides(cols_n, sides, part, first, count, ext, row, on=None):
    me = lax.axis_index("col")
    wide = ext.shape[1]
    for here, at, ref in ((me > 0, 0, sides[0]), (me < cols_n - 1, wide - TILE, sides[-1])):
        there = ref[pl.ds(part * RR + first, count)]
        here = here if on is None else here & on
        ext[pl.ds(row, count), at : at + TILE, :] = jnp.where(here, there, jnp.zeros_like(there))


def spread(ext, cat, width):
    br = ext.shape[-1]
    for b in range(3):
        left = TILE - RC + b * RC
        cat[:, :, b * br : (b + 1) * br] = ext[:, left : left + width, :]


def conv_early(groups, rows_n, cols_n, height, w, *refs):
    g = len(groups)
    ones, twos = refs[:g], refs[g : 2 * g]
    near, far = refs[2 * g : 2 * g + 2]
    sides = refs[2 * g + 2 : -3]
    partial, ext, cat = refs[-3:]
    width = cat.shape[1]
    rest = height - RR
    top = near_is_top()
    for i, (cols, near_first) in enumerate(groups):
        up = top_of(near_first)
        skip = up * (RR - rest)
        rows = [(0, ones[i], 0, RR, RR + (1 - up) * rest, None), (1, twos[i], skip, rest, RR + up * RR, None)]
        if i == 0:
            rows += [(2, near, 0, RR, (1 - top) * (RR + height), None)]
            rows += [(3, far, 0, RR, top * (RR + height), far_inside(rows_n))]
        for part, src, first, count, row, on in rows:
            place(cols, src, first, count, ext, row, on)
            if i == 0:
                place_sides(cols_n, sides, part, first, count, ext, row, on)
    for cols, _ in groups[1:]:
        for col in cols:
            at = (1 + col) * TILE
            zero = jnp.zeros((RR, TILE, ext.shape[2]), BF16)
            ext[0:RR, at : at + TILE, :] = zero
            ext[RR + height :, at : at + TILE, :] = zero
    spread(ext, cat, width)
    k = cat.shape[2]
    for at, count in blocks_of(height):
        total = None
        for a in range(3):
            taps = cat[at + a * RR : at + a * RR + count].reshape(count * width, k)
            term = jnp.dot(taps, w[a * k : (a + 1) * k, :], preferred_element_type=F32)
            total = term if total is None else total + term
        partial[at : at + count] = total.reshape(count, width, total.shape[1])


def far_inside(rows_n):
    me = lax.axis_index("row")
    return (me > 0) & (me < rows_n - 1)


def conv_late(groups, rows_n, height, w, partial, *refs):
    g = len(groups) - 1
    near, far = refs[:g], refs[g : 2 * g]
    out, apart, done, sems = refs[-4:]
    top = near_is_top()
    width, br = partial.shape[1:]
    used = sorted(col for cols, _ in groups[1:] for col in cols)
    lo, hi = used[0] * TILE, (used[-1] + 1) * TILE
    zero = jnp.zeros((2 * RR, TILE, br), F32)
    for b in range(3):
        apart[b, :, 0:TILE, :] = zero
        apart[b, :, TILE + hi - lo : 2 * TILE + hi - lo, :] = zero
    for halo, row, a, on in ((near, (1 - top) * RR, (1 - top) * 2, None), (far, top * RR, top * 2, far_inside(rows_n))):
        for i, (cols, _) in enumerate(groups[1:]):
            there = halo[i][...]
            if on is not None:
                there = jnp.where(on, there, jnp.zeros_like(there))
            there = there.reshape(RR * len(cols) * TILE, br)
            for b in range(3):
                tap = w[pl.ds(pl.multiple_of((3 * a + b) * br, br), br), :]
                term = jnp.dot(there, tap, preferred_element_type=F32).reshape(RR, len(cols) * TILE, br)
                for j, col in enumerate(cols):
                    at = (1 + col) * TILE - lo
                    apart[b, pl.ds(row, RR), at : at + TILE, :] = term[:, j * TILE : (j + 1) * TILE, :]
    reach = []
    for b in range(3):
        shift = (b - 1) * RC
        reach.append((max(0, lo - shift) // TILE * TILE, min(width, -(-(hi - shift) // TILE) * TILE)))
    cuts = sorted({0, width, *[edge for span_b in reach for edge in span_b]})
    copies = []
    for n, (at, count) in enumerate(blocks_of(height)):
        for left, right in zip(cuts, cuts[1:]):
            total = partial[at : at + count, left:right, :]
            for row in (at if at < RR else -1, at - height + 2 * RR if at >= height - RR else -1):
                for b in range(3):
                    if row >= 0 and reach[b][0] <= left and right <= reach[b][1]:
                        first = left + (b - 1) * RC + TILE - lo
                        total = total + apart[b, row : row + count, first : first + right - left, :]
            done[at : at + count, left:right, :] = jnp.maximum(total, 0).astype(BF16)
        copies.append(pltpu.make_async_copy(done.at[pl.ds(at, count)], out.at[pl.ds(at, count)], sems.at[n]))
        copies[-1].start()
    for copy in copies:
        copy.wait()


def blocks_of(height):
    rest = height - RR
    cuts = [0, rest // 2, rest, RR, RR + rest // 2, height]
    return [(lo, hi - lo) for lo, hi in zip(cuts, cuts[1:]) if hi > lo]


def plan(tile_cols):
    groups = [([0, tile_cols - 1], True), (list(range(1, tile_cols - 1)), True)]
    order = [(0, True), (0, False), (1, True), (1, False)]
    return groups, order


def shards(features, assignment, w_reduce, w_expand, w_short, w_branch, w_dilated):
    tile_rows, tile_cols, pixels, channels = features.shape
    mid, cout, br = w_reduce.shape[1], w_expand.shape[1], w_branch.shape[1]
    height, width = tile_rows * TILE, tile_cols * TILE
    assert tile_rows == 2 and pixels == TILE * TILE and TILE < RR <= height <= 2 * RR
    groups, order = plan(tile_cols)
    chunks = [(groups[i][0], one, groups[i][1]) for i, one in order]
    sizes = [span(c, height) * len(c[0]) for c in chunks]
    starts = [sum(sizes[:i]) for i in range(len(sizes))]
    per_row = 2 * (channels * mid + mid * cout + channels * cout + cout * br)
    n_copies = sum(len(list(sources(c, 0))) for c in chunks) + 2 + 3 * (cout // BLOCK)

    def grid_of(cols):
        return jax.ShapeDtypeStruct((RR, len(cols) * TILE, br), BF16)

    first, xs, wr, we, ws, wb = pl.pallas_call(
        functools.partial(first_chunk, chunks, height),
        out_shape=[
            grid_of(chunks[0][0]),
            jax.ShapeDtypeStruct((sum(sizes), channels), BF16),
            jax.ShapeDtypeStruct(w_reduce.shape, BF16),
            jax.ShapeDtypeStruct(w_expand.shape, BF16),
            jax.ShapeDtypeStruct(w_short.shape, BF16),
            jax.ShapeDtypeStruct(w_branch.shape, BF16),
        ],
        in_specs=[HBM] * 6,
        out_specs=[VM] * 6,
        scratch_shapes=[pltpu.SMEM(assignment.shape, jnp.int32), pltpu.SemaphoreType.DMA((n_copies,))],
        compiler_params=params(TRUNK_MIB),
        cost_estimate=cost(per_row * sizes[0], 12 * MIB),
        name="trunk_first",
    )(*[in_hbm(v) for v in (assignment, features, w_reduce, w_expand, w_short, w_branch)])

    rows_n, cols_n = lax.axis_size("row"), lax.axis_size("col")
    assert rows_n % 2 == 0 and cols_n % 2 == 0

    def partner(row, col, near):
        if near:
            return row ^ 1, col
        if row in (0, rows_n - 1):
            return row, col ^ 1
        return (row + 1 if row % 2 else row - 1), col

    def swap(near):
        pairs = []
        for row in range(rows_n):
            for col in range(cols_n):
                to_row, to_col = partner(row, col, near)
                pairs.append((row * cols_n + col, to_row * cols_n + to_col))
        return pairs

    local, halo = {}, {}
    for n, (i, one) in enumerate(order):
        if n == 0:
            value = first
        else:
            extra = [] if one else [local[i, True]]
            value = pl.pallas_call(
                functools.partial(later_chunk, chunks[n], starts[n], height),
                out_shape=grid_of(groups[i][0]),
                in_specs=[SM] + [VM] * (5 + len(extra)),
                out_specs=VM,
                compiler_params=params(TRUNK_MIB),
                cost_estimate=cost(per_row * sizes[n], MIB),
            )(assignment, xs, wr, we, ws, wb, *extra)
        local[i, one] = value
        near = one == groups[i][1]
        halo[i, near] = lax.ppermute(value, ("row", "col"), swap(near))

    side = jax.ShapeDtypeStruct((4 * RR, TILE, br), BF16)
    one_swap = cols_n == 2
    picked = pl.pallas_call(
        functools.partial(pick_kernel, cols_n),
        out_shape=[side] if one_swap else [side, side],
        in_specs=[VM] * 4,
        out_specs=[VM] * (1 if one_swap else 2),
        compiler_params=params(4),
        cost_estimate=cost(0, MIB),
        name="pick",
    )(local[0, True], local[0, False], halo[0, True], halo[0, False])
    if one_swap:
        sides = [lax.ppermute(picked[0], "col", [(0, 1), (1, 0)])]
    else:
        sides = [
            lax.ppermute(picked[0], "col", [(i, i + 1) for i in range(cols_n - 1)]),
            lax.ppermute(picked[1], "col", [(i + 1, i) for i in range(cols_n - 1)]),
        ]

    taps = w_dilated.reshape(9 * br, br)
    n_groups = len(groups)
    pick = lambda table, key: [table[i, key] for i in range(n_groups)]
    flops = 2 * width * 3 * br * br
    edge_halos = [halo[0, True], halo[0, False]]
    partial = pl.pallas_call(
        functools.partial(conv_early, groups, rows_n, cols_n, height),
        out_shape=jax.ShapeDtypeStruct((height, width, br), F32),
        in_specs=[VM] * (3 + 2 * n_groups + len(sides)),
        out_specs=VM,
        scratch_shapes=[
            pltpu.VMEM((height + 2 * RR, width + 2 * TILE, br), BF16),
            pltpu.VMEM((height + 2 * RR, width, 3 * br), BF16),
        ],
        compiler_params=params(CONV_MIB),
        cost_estimate=cost(flops * 3 * height, 4 * MIB),
        name="conv_early",
    )(taps, *pick(local, True), *pick(local, False), *edge_halos, *sides)
    inner = sum(len(cols) for cols, _ in groups[1:]) * TILE
    return pl.pallas_call(
        functools.partial(conv_late, groups, rows_n, height),
        out_shape=jax.ShapeDtypeStruct((height, width, br), BF16),
        in_specs=[VM] * (2 * n_groups),
        out_specs=HBM,
        scratch_shapes=[
            pltpu.VMEM((3, 2 * RR, inner + 2 * TILE, br), F32),
            pltpu.VMEM((height, width, br), BF16),
            pltpu.SemaphoreType.DMA((len(blocks_of(height)),)),
        ],
        compiler_params=params(CONV_MIB),
        cost_estimate=cost(flops * RR, 4 * MIB),
        name="conv_late",
    )(taps, partial, *pick(halo, True)[1:], *pick(halo, False)[1:])


def solution(mesh):
    in_specs = (
        P(("groups", "row"), "col", None, None),
        P(("groups", "row"), "col"),
        P(),
        P(),
        P(),
        P(),
        P(),
    )
    out_specs = P(("groups", "row"), "col", None)

    return jax.shard_map(shards, mesh=mesh, in_specs=in_specs, out_specs=out_specs, check_vma=False)
```

```python
import functools

import jax
import jax.numpy as jnp
from jax import lax
from jax.experimental import pallas as pl
from jax.experimental.pallas import tpu as pltpu
from jax.sharding import PartitionSpec as P


TILE = 16
RR = 18
RC = 15
BLOCK = 512
DEPTH = 3
WAITS = (1, 3)
LATE = 2
F32 = jnp.float32
BF16 = jnp.bfloat16
VM = pl.BlockSpec(memory_space=pltpu.VMEM)
SM = pl.BlockSpec(memory_space=pltpu.SMEM)
HBM = pl.BlockSpec(memory_space=pltpu.MemorySpace.HBM)
MIB = 1 << 20
TRUNK_MIB = 16
CONV_MIB = 24


def params(mib):
    return pltpu.CompilerParams(vmem_limit_bytes=mib * MIB)


def cost(flops, nbytes):
    return pl.CostEstimate(flops=int(flops), bytes_accessed=int(nbytes), transcendentals=0)


def in_hbm(value):
    return pltpu.with_memory_space_constraint(value, pltpu.MemorySpace.HBM)


def near_is_top():
    return lax.rem(lax.axis_index("row"), 2)


def top_of(near_first):
    return near_is_top() if near_first else 1 - near_is_top()


def columns_of(chunk):
    return chunk[0]


def span(chunk, height):
    return (RR if chunk[1] else height - RR) * TILE


def sources(chunk, top):
    rest = (RR - TILE) * TILE
    pixels = TILE * TILE
    for j, col in enumerate(chunk[0]):
        if chunk[1]:
            at = j * (pixels + rest)
            yield 1 - top, col, 0, pixels, at
            yield top, col, (1 - top) * (pixels - rest), rest, at + pixels
        else:
            yield top, col, top * rest, pixels - rest, j * (pixels - rest)


def trunk_rows(x, wr, we, ws, wb, ready=lambda k: None):
    ready(0)
    hidden = jnp.maximum(jnp.dot(x, wr[...], preferred_element_type=F32), 0).astype(BF16)
    total = None
    for k, at in enumerate(range(0, we.shape[1], BLOCK)):
        ready(1 + k)
        summed = jnp.dot(hidden, we[:, at : at + BLOCK], preferred_element_type=F32)
        summed = summed + jnp.dot(x, ws[:, at : at + BLOCK], preferred_element_type=F32)
        block_out = jnp.maximum(summed, 0).astype(BF16)
        term = jnp.dot(block_out, wb[at : at + BLOCK, :], preferred_element_type=F32)
        total = term if total is None else total + term
    return jnp.maximum(total, 0)


def put_column(part, chunk, col, j, top, flags, out):
    width = part.shape[-1]
    where = pl.ds(j * TILE, TILE)
    own = flags[top, col] >= 0
    if chunk[1]:
        pixels = TILE * TILE
        full = jnp.where(flags[1 - top, col] >= 0, part[:pixels], 0.0).astype(BF16)
        rest = jnp.where(own, part[pixels:], 0.0).astype(BF16)
        out[pl.ds((1 - top) * (RR - TILE), TILE), where, :] = full.reshape(TILE, TILE, width)
        out[pl.ds(top * TILE, RR - TILE), where, :] = rest.reshape(RR - TILE, TILE, width)
    else:
        rows = part.shape[0] // TILE
        part = jnp.where(own, part, 0.0).astype(BF16)
        out[pl.ds(top * (RR - rows), rows), where, :] = part.reshape(rows, TILE, width)


def first_chunk(chunks, height, asg, feats, wr_h, we_h, ws_h, wb_h, out, xs, wr, we, ws, wb, flags, sems):
    steps = [[]]
    steps[0].append((asg, flags))
    at = 0
    later = []
    for i, chunk in enumerate(chunks):
        moves = [
            (feats.at[tr, col, pl.ds(first, count), :], xs.at[pl.ds(at + row, count), :])
            for tr, col, first, count, row in sources(chunk, top_of(chunk[2]))
        ]
        at += span(chunk, height) * len(columns_of(chunk))
        if i == 0:
            steps[0] += moves
        else:
            later += moves
    steps[0].append((wr_h, wr))
    ends = [sum(WAITS[: i + 1]) for i in range(len(WAITS))]
    first_of = {}
    for i, n_blocks in enumerate(WAITS):
        first_of[1 + ends[i] - n_blocks] = 1 + i
        cols = pl.ds((ends[i] - n_blocks) * BLOCK, n_blocks * BLOCK)
        steps.append(
            [(ws_h.at[:, cols], ws.at[:, cols]), (we_h.at[:, cols], we.at[:, cols]), (wb_h.at[cols, :], wb.at[cols, :])]
        )
    n_weights = len(steps)
    steps.append(later)
    copies = []
    used = 0
    for step in steps:
        copies.append([pltpu.make_async_copy(src, dst, sems.at[used + j]) for j, (src, dst) in enumerate(step)])
        used += len(step)

    def begin(k):
        if k < len(copies):
            for copy in copies[k]:
                copy.start()

    def ready(k):
        for copy in copies[k]:
            copy.wait()
        begin(k + DEPTH)

    for k in range(DEPTH):
        begin(k)
    ready(0)
    per = span(chunks[0], height)
    cols = columns_of(chunks[0])
    reduced = trunk_rows(xs[0 : per * len(cols), :], wr, we, ws, wb, lambda k: ready(first_of[k]) if k in first_of else None)
    for j, col in enumerate(cols):
        put_column(reduced[j * per : (j + 1) * per], chunks[0], col, j, top_of(chunks[0][2]), flags, out)
    for k in range(n_weights, len(copies)):
        ready(k)


def later_chunk(chunk, at, height, flags, xs, wr, we, ws, wb, *refs):
    out = refs[-1]
    top = top_of(chunk[2])
    per = span(chunk, height)
    cols = columns_of(chunk)

    def busy(col):
        own = flags[top, col] >= 0
        if chunk[1]:
            own = own | (flags[1 - top, col] >= 0)
        return own

    active = [busy(col) for col in cols]
    every = functools.reduce(lambda a, b: a & b, active)
    zero = jnp.zeros((span(chunk, height), out.shape[-1]), F32)

    @pl.when(every)
    def _():
        reduced = trunk_rows(xs[at : at + per * len(cols), :], wr, we, ws, wb)
        for j, col in enumerate(cols):
            put_column(reduced[j * per : (j + 1) * per], chunk, col, j, top, flags, out)

    if len(cols) == 1:
        @pl.when(jnp.logical_not(every))
        def _():
            put_column(zero, chunk, cols[0], 0, top, flags, out)
    else:
        for j, col in enumerate(cols):
            @pl.when(jnp.logical_not(active[j]))
            def _():
                put_column(zero, chunk, col, j, top, flags, out)

        one = cols[0]
        step = cols[1] - cols[0]

        @pl.loop(0, len(cols))
        def _(j):
            col = one + j * step
            mine = flags[top, col] >= 0
            if chunk[1]:
                mine = mine | (flags[1 - top, col] >= 0)

            @pl.when(mine & jnp.logical_not(every))
            def _():
                rows = pl.ds(pl.multiple_of(at + j * per, TILE), per)
                put_column(trunk_rows(xs[rows, :], wr, we, ws, wb), chunk, col, j, top, flags, out)

    if not chunk[1]:
        near = refs[0]
        shared = 2 * RR - height
        out[pl.ds((1 - top) * (RR - shared), shared)] = near[pl.ds(top * (RR - shared), shared)]


def pick_kernel(cols_n, *refs):
    n = 1 if cols_n == 2 else 2
    ins, outs = refs[:-n], refs[-n:]
    width = ins[0].shape[1]
    for i, src in enumerate(ins):
        rows = pl.ds(i * RR, RR)
        if cols_n == 2:
            first = pl.multiple_of((1 - lax.axis_index("col")) * (width - TILE), TILE)
            outs[0][rows] = src[:, pl.ds(first, TILE), :]
        else:
            outs[0][rows] = src[:, width - TILE :, :]
            outs[1][rows] = src[:, :TILE, :]


def place(cols, src, first, count, ext, row, on=None):
    for j, col in enumerate(cols):
        there = src[pl.ds(first, count), j * TILE : (j + 1) * TILE, :]
        if on is not None:
            there = jnp.where(on, there, jnp.zeros_like(there))
        ext[pl.ds(row, count), (1 + col) * TILE : (2 + col) * TILE, :] = there


def place_sides(cols_n, sides, part, first, count, ext, row, on=None):
    me = lax.axis_index("col")
    wide = ext.shape[1]
    for here, at, ref in ((me > 0, 0, sides[0]), (me < cols_n - 1, wide - TILE, sides[-1])):
        there = ref[pl.ds(part * RR + first, count)]
        here = here if on is None else here & on
        ext[pl.ds(row, count), at : at + TILE, :] = jnp.where(here, there, jnp.zeros_like(there))


def spread(ext, cat, width):
    br = ext.shape[-1]
    for b in range(3):
        left = TILE - RC + b * RC
        cat[:, :, b * br : (b + 1) * br] = ext[:, left : left + width, :]


def conv_early(groups, rows_n, cols_n, height, w, *refs):
    g = len(groups)
    ones, twos, far = refs[:g], refs[g : 2 * g], refs[2 * g : 3 * g]
    near = refs[3 * g]
    sides = refs[3 * g + 1 : -6]
    out, partial, ext, cat, done, sem = refs[-6:]
    width = cat.shape[1]
    rest = height - RR
    top = near_is_top()
    near_row = (1 - top) * (RR + height)
    for i, (cols, near_first) in enumerate(groups):
        up = top_of(near_first)
        skip = up * (RR - rest)
        rows = [(0, ones[i], 0, RR, RR + (1 - up) * rest, None), (1, twos[i], skip, rest, RR + up * RR, None)]
        rows += [(3, far[i], 0, RR, top * (RR + height), far_inside(rows_n))]
        if i == 0:
            rows += [(2, near, 0, RR, near_row, None)]
        for part, src, first, count, row, on in rows:
            place(cols, src, first, count, ext, row, on)
            if i == 0:
                place_sides(cols_n, sides, part, first, count, ext, row, on)
    for cols, _ in groups[1:]:
        for col in cols:
            ext[pl.ds(near_row, RR), (1 + col) * TILE : (2 + col) * TILE, :] = jnp.zeros((RR, TILE, ext.shape[2]), BF16)
    spread(ext, cat, width)
    k = cat.shape[2]
    for at, count in blocks_of(height):
        total = None
        for a in range(3):
            taps = cat[at + a * RR : at + a * RR + count].reshape(count * width, k)
            term = jnp.dot(taps, w[a * k : (a + 1) * k, :], preferred_element_type=F32)
            total = term if total is None else total + term
        partial[at : at + count] = total.reshape(count, width, total.shape[1])
    rows = pl.ds(top * RR, rest)
    done[...] = jnp.maximum(partial[rows], 0).astype(BF16)
    copy = pltpu.make_async_copy(done, out.at[rows], sem)
    copy.start()
    copy.wait()


def far_inside(rows_n):
    me = lax.axis_index("row")
    return (me > 0) & (me < rows_n - 1)


def conv_late(groups, height, w, partial, *refs):
    near = refs[: len(groups) - 1]
    _, out, apart, done, sems = refs[-5:]
    top = near_is_top()
    width, br = partial.shape[1:]
    rest = height - RR
    used = sorted(col for cols, _ in groups[1:] for col in cols)
    lo, hi = used[0] * TILE, (used[-1] + 1) * TILE
    reach = []
    for b in range(3):
        shift = (b - 1) * RC
        reach.append((max(0, lo - shift) // TILE * TILE, min(width, -(-(hi - shift) // TILE) * TILE)))
    cuts = sorted({0, width, *[edge for span_b in reach for edge in span_b]})
    zero = jnp.zeros((RR, TILE, br), F32)
    for b in range(3):
        apart[b, :, 0:TILE, :] = zero
        apart[b, :, TILE + hi - lo : 2 * TILE + hi - lo, :] = zero
    for i, (cols, _) in enumerate(groups[1:]):
        there = near[i][...].reshape(RR * len(cols) * TILE, br)
        for b in range(3):
            tap = w[pl.ds(pl.multiple_of((6 * (1 - top) + b) * br, br), br), :]
            term = jnp.dot(there, tap, preferred_element_type=F32).reshape(RR, len(cols) * TILE, br)
            for j, col in enumerate(cols):
                at = (1 + col) * TILE - lo
                apart[b, :, at : at + TILE, :] = term[:, j * TILE : (j + 1) * TILE, :]
    copies = []
    step = RR // LATE
    for at in range(0, RR, step):
        rows = pl.ds((1 - top) * rest + at, step)
        for left, right in zip(cuts, cuts[1:]):
            total = partial[rows, left:right, :]
            for b in range(3):
                if reach[b][0] <= left and right <= reach[b][1]:
                    first = left + (b - 1) * RC + TILE - lo
                    total = total + apart[b, at : at + step, first : first + right - left, :]
            done[at : at + step, left:right, :] = jnp.maximum(total, 0).astype(BF16)
        copies.append(pltpu.make_async_copy(done.at[pl.ds(at, step)], out.at[rows], sems.at[len(copies)]))
        copies[-1].start()
    for copy in copies:
        copy.wait()


def blocks_of(height):
    rest = height - RR
    cuts = [0, rest // 2, rest, RR, RR + rest // 2, height]
    return [(lo, hi - lo) for lo, hi in zip(cuts, cuts[1:]) if hi > lo]


def plan(tile_cols):
    groups = [([0, tile_cols - 1], True), (list(range(1, tile_cols - 1)), False)]
    order = [(0, True), (0, False), (1, True), (1, False)]
    return groups, order


def shards(features, assignment, w_reduce, w_expand, w_short, w_branch, w_dilated):
    tile_rows, tile_cols, pixels, channels = features.shape
    mid, cout, br = w_reduce.shape[1], w_expand.shape[1], w_branch.shape[1]
    height, width = tile_rows * TILE, tile_cols * TILE
    assert tile_rows == 2 and pixels == TILE * TILE and TILE < RR <= height <= 2 * RR
    groups, order = plan(tile_cols)
    chunks = [(groups[i][0], one, groups[i][1]) for i, one in order]
    sizes = [span(c, height) * len(c[0]) for c in chunks]
    starts = [sum(sizes[:i]) for i in range(len(sizes))]
    per_row = 2 * (channels * mid + mid * cout + channels * cout + cout * br)
    n_copies = sum(len(list(sources(c, 0))) for c in chunks) + 2 + 3 * (cout // BLOCK)

    def grid_of(cols):
        return jax.ShapeDtypeStruct((RR, len(cols) * TILE, br), BF16)

    first, xs, wr, we, ws, wb = pl.pallas_call(
        functools.partial(first_chunk, chunks, height),
        out_shape=[
            grid_of(chunks[0][0]),
            jax.ShapeDtypeStruct((sum(sizes), channels), BF16),
            jax.ShapeDtypeStruct(w_reduce.shape, BF16),
            jax.ShapeDtypeStruct(w_expand.shape, BF16),
            jax.ShapeDtypeStruct(w_short.shape, BF16),
            jax.ShapeDtypeStruct(w_branch.shape, BF16),
        ],
        in_specs=[HBM] * 6,
        out_specs=[VM] * 6,
        scratch_shapes=[pltpu.SMEM(assignment.shape, jnp.int32), pltpu.SemaphoreType.DMA((n_copies,))],
        compiler_params=params(TRUNK_MIB),
        cost_estimate=cost(per_row * sizes[0], 12 * MIB),
        name="trunk_first",
    )(*[in_hbm(v) for v in (assignment, features, w_reduce, w_expand, w_short, w_branch)])

    rows_n, cols_n = lax.axis_size("row"), lax.axis_size("col")
    assert rows_n % 2 == 0 and cols_n % 2 == 0

    def partner(row, col, near):
        if near:
            return row ^ 1, col
        if row in (0, rows_n - 1):
            return row, col ^ 1
        return (row + 1 if row % 2 else row - 1), col

    def swap(near):
        pairs = []
        for row in range(rows_n):
            for col in range(cols_n):
                to_row, to_col = partner(row, col, near)
                pairs.append((row * cols_n + col, to_row * cols_n + to_col))
        return pairs

    local, halo = {}, {}
    for n, (i, one) in enumerate(order):
        if n == 0:
            value = first
        else:
            extra = [] if one else [local[i, True]]
            value = pl.pallas_call(
                functools.partial(later_chunk, chunks[n], starts[n], height),
                out_shape=grid_of(groups[i][0]),
                in_specs=[SM] + [VM] * (5 + len(extra)),
                out_specs=VM,
                compiler_params=params(TRUNK_MIB),
                cost_estimate=cost(per_row * sizes[n], MIB),
            )(assignment, xs, wr, we, ws, wb, *extra)
        local[i, one] = value
        near = one == groups[i][1]
        halo[i, near] = lax.ppermute(value, ("row", "col"), swap(near))

    side = jax.ShapeDtypeStruct((4 * RR, TILE, br), BF16)
    one_swap = cols_n == 2
    picked = pl.pallas_call(
        functools.partial(pick_kernel, cols_n),
        out_shape=[side] if one_swap else [side, side],
        in_specs=[VM] * 4,
        out_specs=[VM] * (1 if one_swap else 2),
        compiler_params=params(4),
        cost_estimate=cost(0, MIB),
        name="pick",
    )(local[0, True], local[0, False], halo[0, True], halo[0, False])
    if one_swap:
        sides = [lax.ppermute(picked[0], "col", [(0, 1), (1, 0)])]
    else:
        sides = [
            lax.ppermute(picked[0], "col", [(i, i + 1) for i in range(cols_n - 1)]),
            lax.ppermute(picked[1], "col", [(i + 1, i) for i in range(cols_n - 1)]),
        ]

    taps = w_dilated.reshape(9 * br, br)
    rest = height - RR
    n_groups = len(groups)
    pick = lambda table, key: [table[i, key] for i in range(n_groups)]
    flops = 2 * width * 3 * br * br
    out, partial = pl.pallas_call(
        functools.partial(conv_early, groups, rows_n, cols_n, height),
        out_shape=[
            jax.ShapeDtypeStruct((height, width, br), BF16),
            jax.ShapeDtypeStruct((height, width, br), F32),
        ],
        in_specs=[VM] * (2 + 3 * n_groups + len(sides)),
        out_specs=[HBM, VM],
        scratch_shapes=[
            pltpu.VMEM((height + 2 * RR, width + 2 * TILE, br), BF16),
            pltpu.VMEM((height + 2 * RR, width, 3 * br), BF16),
            pltpu.VMEM((rest, width, br), BF16),
            pltpu.SemaphoreType.DMA,
        ],
        compiler_params=params(CONV_MIB),
        cost_estimate=cost(flops * 3 * height, 4 * MIB),
        name="conv_early",
    )(taps, *pick(local, True), *pick(local, False), *pick(halo, False), halo[0, True], *sides)
    inner = sum(len(cols) for cols, _ in groups[1:]) * TILE
    return pl.pallas_call(
        functools.partial(conv_late, groups, height),
        out_shape=jax.ShapeDtypeStruct((height, width, br), BF16),
        in_specs=[VM] * (1 + n_groups) + [HBM],
        out_specs=HBM,
        input_output_aliases={1 + n_groups: 0},
        scratch_shapes=[
            pltpu.VMEM((3, RR, inner + 2 * TILE, br), F32),
            pltpu.VMEM((RR, width, br), BF16),
            pltpu.SemaphoreType.DMA((LATE,)),
        ],
        compiler_params=params(CONV_MIB),
        cost_estimate=cost(flops * RR, 4 * MIB),
        name="conv_late",
    )(taps, partial, *pick(halo, True)[1:], out)


def solution(mesh):
    in_specs = (
        P(("groups", "row"), "col", None, None),
        P(("groups", "row"), "col"),
        P(),
        P(),
        P(),
        P(),
        P(),
    )
    out_specs = P(("groups", "row"), "col", None)

    return jax.shard_map(shards, mesh=mesh, in_specs=in_specs, out_specs=out_specs, check_vma=False)
```

```python
import functools

import jax
import jax.numpy as jnp
from jax import lax
from jax.experimental import pallas as pl
from jax.experimental.pallas import tpu as pltpu
from jax.sharding import PartitionSpec as P


TILE = 16
RR = 18
RC = 15
BLOCK = 512
DEPTH = 3
WAITS = (1, 3)
LATE = 2
F32 = jnp.float32
BF16 = jnp.bfloat16
VM = pl.BlockSpec(memory_space=pltpu.VMEM)
SM = pl.BlockSpec(memory_space=pltpu.SMEM)
HBM = pl.BlockSpec(memory_space=pltpu.MemorySpace.HBM)
MIB = 1 << 20
TRUNK_MIB = 16
CONV_MIB = 24


def params(mib):
    return pltpu.CompilerParams(vmem_limit_bytes=mib * MIB)


def cost(flops, nbytes):
    return pl.CostEstimate(flops=int(flops), bytes_accessed=int(nbytes), transcendentals=0)


def in_hbm(value):
    return pltpu.with_memory_space_constraint(value, pltpu.MemorySpace.HBM)


def near_is_top():
    return lax.rem(lax.axis_index("row"), 2)


def top_of(near_first):
    return near_is_top() if near_first else 1 - near_is_top()


def columns_of(chunk):
    return chunk[0]


def span(chunk, height):
    return (RR if chunk[1] else height - RR) * TILE


def sources(chunk, top):
    rest = (RR - TILE) * TILE
    pixels = TILE * TILE
    for j, col in enumerate(chunk[0]):
        if chunk[1]:
            at = j * (pixels + rest)
            yield 1 - top, col, 0, pixels, at
            yield top, col, (1 - top) * (pixels - rest), rest, at + pixels
        else:
            yield top, col, top * rest, pixels - rest, j * (pixels - rest)


def trunk_rows(x, wr, we, ws, wb, ready=lambda k: None):
    ready(0)
    hidden = jnp.maximum(jnp.dot(x, wr[...], preferred_element_type=F32), 0).astype(BF16)
    total = None
    for k, at in enumerate(range(0, we.shape[1], BLOCK)):
        ready(1 + k)
        summed = jnp.dot(hidden, we[:, at : at + BLOCK], preferred_element_type=F32)
        summed = summed + jnp.dot(x, ws[:, at : at + BLOCK], preferred_element_type=F32)
        block_out = jnp.maximum(summed, 0).astype(BF16)
        term = jnp.dot(block_out, wb[at : at + BLOCK, :], preferred_element_type=F32)
        total = term if total is None else total + term
    return jnp.maximum(total, 0)


def put_column(part, chunk, col, j, top, flags, out):
    width = part.shape[-1]
    where = pl.ds(j * TILE, TILE)
    own = flags[top, col] >= 0
    if chunk[1]:
        pixels = TILE * TILE
        full = jnp.where(flags[1 - top, col] >= 0, part[:pixels], 0.0).astype(BF16)
        rest = jnp.where(own, part[pixels:], 0.0).astype(BF16)
        out[pl.ds((1 - top) * (RR - TILE), TILE), where, :] = full.reshape(TILE, TILE, width)
        out[pl.ds(top * TILE, RR - TILE), where, :] = rest.reshape(RR - TILE, TILE, width)
    else:
        rows = part.shape[0] // TILE
        part = jnp.where(own, part, 0.0).astype(BF16)
        out[pl.ds(top * (RR - rows), rows), where, :] = part.reshape(rows, TILE, width)


def first_chunk(chunks, height, asg, feats, wr_h, we_h, ws_h, wb_h, out, xs, wr, we, ws, wb, flags, sems):
    steps = [[]]
    steps[0].append((asg, flags))
    at = 0
    later = []
    for i, chunk in enumerate(chunks):
        moves = [
            (feats.at[tr, col, pl.ds(first, count), :], xs.at[pl.ds(at + row, count), :])
            for tr, col, first, count, row in sources(chunk, top_of(chunk[2]))
        ]
        at += span(chunk, height) * len(columns_of(chunk))
        if i == 0:
            steps[0] += moves
        else:
            later += moves
    steps[0].append((wr_h, wr))
    ends = [sum(WAITS[: i + 1]) for i in range(len(WAITS))]
    first_of = {}
    for i, n_blocks in enumerate(WAITS):
        first_of[1 + ends[i] - n_blocks] = 1 + i
        cols = pl.ds((ends[i] - n_blocks) * BLOCK, n_blocks * BLOCK)
        steps.append(
            [(ws_h.at[:, cols], ws.at[:, cols]), (we_h.at[:, cols], we.at[:, cols]), (wb_h.at[cols, :], wb.at[cols, :])]
        )
    n_weights = len(steps)
    steps.append(later)
    copies = []
    used = 0
    for step in steps:
        copies.append([pltpu.make_async_copy(src, dst, sems.at[used + j]) for j, (src, dst) in enumerate(step)])
        used += len(step)

    def begin(k):
        if k < len(copies):
            for copy in copies[k]:
                copy.start()

    def ready(k):
        for copy in copies[k]:
            copy.wait()
        begin(k + DEPTH)

    for k in range(DEPTH):
        begin(k)
    ready(0)
    per = span(chunks[0], height)
    cols = columns_of(chunks[0])
    reduced = trunk_rows(xs[0 : per * len(cols), :], wr, we, ws, wb, lambda k: ready(first_of[k]) if k in first_of else None)
    for j, col in enumerate(cols):
        put_column(reduced[j * per : (j + 1) * per], chunks[0], col, j, top_of(chunks[0][2]), flags, out)
    for k in range(n_weights, len(copies)):
        ready(k)


def later_chunk(chunk, at, height, flags, xs, wr, we, ws, wb, *refs):
    out = refs[-1]
    top = top_of(chunk[2])
    per = span(chunk, height)
    cols = columns_of(chunk)

    def busy(col):
        own = flags[top, col] >= 0
        if chunk[1]:
            own = own | (flags[1 - top, col] >= 0)
        return own

    active = [busy(col) for col in cols]
    every = functools.reduce(lambda a, b: a & b, active)
    zero = jnp.zeros((span(chunk, height), out.shape[-1]), F32)

    @pl.when(every)
    def _():
        reduced = trunk_rows(xs[at : at + per * len(cols), :], wr, we, ws, wb)
        for j, col in enumerate(cols):
            put_column(reduced[j * per : (j + 1) * per], chunk, col, j, top, flags, out)

    if len(cols) == 1:
        @pl.when(jnp.logical_not(every))
        def _():
            put_column(zero, chunk, cols[0], 0, top, flags, out)
    else:
        for j, col in enumerate(cols):
            @pl.when(jnp.logical_not(active[j]))
            def _():
                put_column(zero, chunk, col, j, top, flags, out)

        one = cols[0]
        step = cols[1] - cols[0]

        @pl.loop(0, len(cols))
        def _(j):
            col = one + j * step
            mine = flags[top, col] >= 0
            if chunk[1]:
                mine = mine | (flags[1 - top, col] >= 0)

            @pl.when(mine & jnp.logical_not(every))
            def _():
                rows = pl.ds(pl.multiple_of(at + j * per, TILE), per)
                put_column(trunk_rows(xs[rows, :], wr, we, ws, wb), chunk, col, j, top, flags, out)

    if not chunk[1]:
        near = refs[0]
        shared = 2 * RR - height
        out[pl.ds((1 - top) * (RR - shared), shared)] = near[pl.ds(top * (RR - shared), shared)]


def pick_kernel(cols_n, used, *refs):
    outs = refs[-(1 if cols_n == 2 else 2) :]
    width = refs[0].shape[1]
    for i, src in enumerate(refs[:used]):
        rows = pl.ds(i * RR, RR)
        if cols_n == 2:
            first = pl.multiple_of((1 - lax.axis_index("col")) * (width - TILE), TILE)
            outs[0][rows] = src[:, pl.ds(first, TILE), :]
        else:
            outs[0][rows] = src[:, width - TILE :, :]
            outs[1][rows] = src[:, :TILE, :]


def place(cols, src, first, count, ext, row, on=None):
    for j, col in enumerate(cols):
        there = src[pl.ds(first, count), j * TILE : (j + 1) * TILE, :]
        if on is not None:
            there = jnp.where(on, there, jnp.zeros_like(there))
        ext[pl.ds(row, count), (1 + col) * TILE : (2 + col) * TILE, :] = there


def place_sides(cols_n, sides, part, first, count, ext, row, on=None):
    me = lax.axis_index("col")
    wide = ext.shape[1]
    for here, at, ref in ((me > 0, 0, sides[0]), (me < cols_n - 1, wide - TILE, sides[-1])):
        there = ref[pl.ds(part * RR + first, count)]
        here = here if on is None else here & on
        ext[pl.ds(row, count), at : at + TILE, :] = jnp.where(here, there, jnp.zeros_like(there))


def spread(ext, cat, width):
    br = ext.shape[-1]
    for b in range(3):
        left = TILE - RC + b * RC
        cat[:, :, b * br : (b + 1) * br] = ext[:, left : left + width, :]


def conv_early(groups, rows_n, cols_n, height, w, *refs):
    g = len(groups)
    ones, twos, far = refs[:g], refs[g : 2 * g], refs[2 * g : 3 * g]
    sides = refs[3 * g : -6]
    out, partial, ext, cat, done, sem = refs[-6:]
    width = cat.shape[1]
    br = ext.shape[2]
    rest = height - RR
    far_top = 1 - near_is_top()
    local = far_top * RR
    for i, (cols, near_first) in enumerate(groups):
        up = top_of(near_first)
        skip = up * (RR - rest)
        rows = [(0, ones[i], 0, RR, local + (1 - up) * rest, None), (1, twos[i], skip, rest, local + up * RR, None)]
        rows += [(2, far[i], 0, RR, (1 - far_top) * height, far_inside(rows_n))]
        for part, src, first, count, row, on in rows:
            place(cols, src, first, count, ext, row, on)
            if i == 0:
                place_sides(cols_n, sides, part, first, count, ext, row, on)
    spread(ext, cat, width)
    k = cat.shape[2]
    total = None
    for a in range(3):
        taps = cat[a * RR : a * RR + rest].reshape(rest * width, k)
        term = jnp.dot(taps, w[a * k : (a + 1) * k, :], preferred_element_type=F32)
        total = term if total is None else total + term
    done[...] = jnp.maximum(total, 0).astype(BF16).reshape(rest, width, br)
    copy = pltpu.make_async_copy(done, out.at[pl.ds((1 - far_top) * RR, rest)], sem)
    copy.start()
    centre = cat[pl.ds(far_top * height, RR)].reshape(RR * width, k)
    inner = cat[pl.ds(far_top * rest + (1 - far_top) * RR, RR)].reshape(RR * width, k)
    inner_w = w[pl.ds(pl.multiple_of((1 - far_top) * 2 * k, k), k), :]
    total = jnp.dot(centre, w[k : 2 * k, :], preferred_element_type=F32) + jnp.dot(
        inner, inner_w, preferred_element_type=F32
    )
    partial[...] = total.reshape(RR, width, br)
    copy.wait()


def far_inside(rows_n):
    me = lax.axis_index("row")
    return (me > 0) & (me < rows_n - 1)


def conv_late(groups, cols_n, height, w, partial, *refs):
    near = refs[: len(groups)]
    sides = refs[len(groups) : -5]
    _, out, apart, done, sems = refs[-5:]
    top = near_is_top()
    width, br = partial.shape[1:]
    rest = height - RR

    def product(value, b):
        tap = w[pl.ds(pl.multiple_of((6 * (1 - top) + b) * br, br), br), :]
        rows, cols = value.shape[:2]
        return jnp.dot(value.reshape(rows * cols, br), tap, preferred_element_type=F32).reshape(rows, cols, br)

    for i, (cols, _) in enumerate(groups):
        for b in range(3):
            term = product(near[i][...], b)
            for j, col in enumerate(cols):
                apart[b, :, (1 + col) * TILE : (2 + col) * TILE, :] = term[:, j * TILE : (j + 1) * TILE, :]
    me = lax.axis_index("col")
    for on, b, at, ref in ((me > 0, 0, 0, sides[0]), (me < cols_n - 1, 2, TILE + width, sides[-1])):
        there = ref[...]
        apart[b, :, at : at + TILE, :] = product(jnp.where(on, there, jnp.zeros_like(there)), b)
    copies = []
    step = RR // LATE
    for at in range(0, RR, step):
        rows = pl.ds(at, step)
        total = partial[rows]
        for b in range(3):
            left = TILE - RC + b * RC
            total = total + apart[b, at : at + step, left : left + width, :]
        done[rows] = jnp.maximum(total, 0).astype(BF16)
        there = out.at[pl.ds((1 - top) * rest + at, step)]
        copies.append(pltpu.make_async_copy(done.at[rows], there, sems.at[len(copies)]))
        copies[-1].start()
    for copy in copies:
        copy.wait()


def plan(tile_cols):
    groups = [([0, tile_cols - 1], False), (list(range(1, tile_cols - 1)), False)]
    order = [(0, True), (0, False), (1, True), (1, False)]
    return groups, order


def shards(features, assignment, w_reduce, w_expand, w_short, w_branch, w_dilated):
    tile_rows, tile_cols, pixels, channels = features.shape
    mid, cout, br = w_reduce.shape[1], w_expand.shape[1], w_branch.shape[1]
    height, width = tile_rows * TILE, tile_cols * TILE
    assert tile_rows == 2 and pixels == TILE * TILE and TILE < RR <= height <= 2 * RR
    groups, order = plan(tile_cols)
    chunks = [(groups[i][0], one, groups[i][1]) for i, one in order]
    sizes = [span(c, height) * len(c[0]) for c in chunks]
    starts = [sum(sizes[:i]) for i in range(len(sizes))]
    per_row = 2 * (channels * mid + mid * cout + channels * cout + cout * br)
    n_copies = sum(len(list(sources(c, 0))) for c in chunks) + 2 + 3 * (cout // BLOCK)

    def grid_of(cols):
        return jax.ShapeDtypeStruct((RR, len(cols) * TILE, br), BF16)

    first, xs, wr, we, ws, wb = pl.pallas_call(
        functools.partial(first_chunk, chunks, height),
        out_shape=[
            grid_of(chunks[0][0]),
            jax.ShapeDtypeStruct((sum(sizes), channels), BF16),
            jax.ShapeDtypeStruct(w_reduce.shape, BF16),
            jax.ShapeDtypeStruct(w_expand.shape, BF16),
            jax.ShapeDtypeStruct(w_short.shape, BF16),
            jax.ShapeDtypeStruct(w_branch.shape, BF16),
        ],
        in_specs=[HBM] * 6,
        out_specs=[VM] * 6,
        scratch_shapes=[pltpu.SMEM(assignment.shape, jnp.int32), pltpu.SemaphoreType.DMA((n_copies,))],
        compiler_params=params(TRUNK_MIB),
        cost_estimate=cost(per_row * sizes[0], 12 * MIB),
        name="trunk_first",
    )(*[in_hbm(v) for v in (assignment, features, w_reduce, w_expand, w_short, w_branch)])

    rows_n, cols_n = lax.axis_size("row"), lax.axis_size("col")
    assert rows_n % 2 == 0 and cols_n % 2 == 0

    def partner(row, col, near):
        if near:
            return row ^ 1, col
        if row in (0, rows_n - 1):
            return row, col ^ 1
        return (row + 1 if row % 2 else row - 1), col

    def swap(near):
        pairs = []
        for row in range(rows_n):
            for col in range(cols_n):
                to_row, to_col = partner(row, col, near)
                pairs.append((row * cols_n + col, to_row * cols_n + to_col))
        return pairs

    local, halo = {}, {}
    for n, (i, one) in enumerate(order):
        if n == 0:
            value = first
        else:
            extra = [] if one else [local[i, True]]
            value = pl.pallas_call(
                functools.partial(later_chunk, chunks[n], starts[n], height),
                out_shape=grid_of(groups[i][0]),
                in_specs=[SM] + [VM] * (5 + len(extra)),
                out_specs=VM,
                compiler_params=params(TRUNK_MIB),
                cost_estimate=cost(per_row * sizes[n], MIB),
            )(assignment, xs, wr, we, ws, wb, *extra)
        local[i, one] = value
        near = one == groups[i][1]
        halo[i, near] = lax.ppermute(value, ("row", "col"), swap(near))

    def trade(arrays, after=()):
        used = len(arrays)
        side = jax.ShapeDtypeStruct((used * RR, TILE, br), BF16)
        n_out = 1 if cols_n == 2 else 2
        picked = pl.pallas_call(
            functools.partial(pick_kernel, cols_n, used),
            out_shape=[side] * n_out,
            in_specs=[VM] * used + [pl.BlockSpec(memory_space=pl.ANY)] * len(after),
            out_specs=[VM] * n_out,
            compiler_params=params(4),
            cost_estimate=cost(0, MIB),
        )(*arrays, *after)
        if cols_n == 2:
            return [lax.ppermute(picked[0], "col", [(0, 1), (1, 0)])]
        return [
            lax.ppermute(picked[0], "col", [(i, i + 1) for i in range(cols_n - 1)]),
            lax.ppermute(picked[1], "col", [(i + 1, i) for i in range(cols_n - 1)]),
        ]

    taps = w_dilated.reshape(9 * br, br)
    rest = height - RR
    n_groups = len(groups)
    pick = lambda table, key: [table[i, key] for i in range(n_groups)]
    flops = 2 * width * 3 * br * br
    sides = trade([local[0, True], local[0, False], halo[0, False]])
    out, partial = pl.pallas_call(
        functools.partial(conv_early, groups, rows_n, cols_n, height),
        out_shape=[
            jax.ShapeDtypeStruct((height, width, br), BF16),
            jax.ShapeDtypeStruct((RR, width, br), F32),
        ],
        in_specs=[VM] * (1 + 3 * n_groups + len(sides)),
        out_specs=[HBM, VM],
        scratch_shapes=[
            pltpu.VMEM((height + RR, width + 2 * TILE, br), BF16),
            pltpu.VMEM((height + RR, width, 3 * br), BF16),
            pltpu.VMEM((rest, width, br), BF16),
            pltpu.SemaphoreType.DMA,
        ],
        compiler_params=params(CONV_MIB),
        cost_estimate=cost(flops * (3 * rest + 2 * RR), 4 * MIB),
        name="conv_early",
    )(taps, *pick(local, True), *pick(local, False), *pick(halo, False), *sides)
    rims = trade([halo[0, True]], [partial])
    n_in = 2 + n_groups + len(rims)
    return pl.pallas_call(
        functools.partial(conv_late, groups, cols_n, height),
        out_shape=jax.ShapeDtypeStruct((height, width, br), BF16),
        in_specs=[VM] * n_in + [HBM],
        out_specs=HBM,
        input_output_aliases={n_in: 0},
        scratch_shapes=[
            pltpu.VMEM((3, RR, width + 2 * TILE, br), F32),
            pltpu.VMEM((RR, width, br), BF16),
            pltpu.SemaphoreType.DMA((LATE,)),
        ],
        compiler_params=params(16),
        cost_estimate=cost(flops * RR, 4 * MIB),
        name="conv_late",
    )(taps, partial, *pick(halo, True), *rims, out)


def solution(mesh):
    in_specs = (
        P(("groups", "row"), "col", None, None),
        P(("groups", "row"), "col"),
        P(),
        P(),
        P(),
        P(),
        P(),
    )
    out_specs = P(("groups", "row"), "col", None)

    return jax.shard_map(shards, mesh=mesh, in_specs=in_specs, out_specs=out_specs, check_vma=False)
```

```python
import functools

import jax
import jax.numpy as jnp
from jax import lax
from jax.experimental import pallas as pl
from jax.experimental.pallas import tpu as pltpu
from jax.sharding import PartitionSpec as P


TILE = 16
RR = 18
RC = 15
BLOCK = 512
DEPTH = 3
WAITS = (1, 3)
LATE = 2
F32 = jnp.float32
BF16 = jnp.bfloat16
VM = pl.BlockSpec(memory_space=pltpu.VMEM)
SM = pl.BlockSpec(memory_space=pltpu.SMEM)
HBM = pl.BlockSpec(memory_space=pltpu.MemorySpace.HBM)
MIB = 1 << 20
TRUNK_MIB = 16
CONV_MIB = 24


def params(mib):
    return pltpu.CompilerParams(vmem_limit_bytes=mib * MIB)


def cost(flops, nbytes):
    return pl.CostEstimate(flops=int(flops), bytes_accessed=int(nbytes), transcendentals=0)


def in_hbm(value):
    return pltpu.with_memory_space_constraint(value, pltpu.MemorySpace.HBM)


def near_is_top():
    return lax.rem(lax.axis_index("row"), 2)


def top_of(near_first):
    return near_is_top() if near_first else 1 - near_is_top()


def columns_of(chunk):
    return chunk[0]


def span(chunk, height):
    return (RR if chunk[1] else height - RR) * TILE


def sources(chunk, top):
    rest = (RR - TILE) * TILE
    pixels = TILE * TILE
    for j, col in enumerate(chunk[0]):
        if chunk[1]:
            at = j * (pixels + rest)
            yield 1 - top, col, 0, pixels, at
            yield top, col, (1 - top) * (pixels - rest), rest, at + pixels
        else:
            yield top, col, top * rest, pixels - rest, j * (pixels - rest)


def trunk_rows(x, wr, we, ws, wb, ready=lambda k: None):
    ready(0)
    hidden = jnp.maximum(jnp.dot(x, wr[...], preferred_element_type=F32), 0).astype(BF16)
    total = None
    for k, at in enumerate(range(0, we.shape[1], BLOCK)):
        ready(1 + k)
        summed = jnp.dot(hidden, we[:, at : at + BLOCK], preferred_element_type=F32)
        summed = summed + jnp.dot(x, ws[:, at : at + BLOCK], preferred_element_type=F32)
        block_out = jnp.maximum(summed, 0).astype(BF16)
        term = jnp.dot(block_out, wb[at : at + BLOCK, :], preferred_element_type=F32)
        total = term if total is None else total + term
    return jnp.maximum(total, 0)


def put_column(part, chunk, col, j, top, flags, out):
    width = part.shape[-1]
    where = pl.ds(j * TILE, TILE)
    own = flags[top, col] >= 0
    if chunk[1]:
        pixels = TILE * TILE
        full = jnp.where(flags[1 - top, col] >= 0, part[:pixels], 0.0).astype(BF16)
        rest = jnp.where(own, part[pixels:], 0.0).astype(BF16)
        out[pl.ds((1 - top) * (RR - TILE), TILE), where, :] = full.reshape(TILE, TILE, width)
        out[pl.ds(top * TILE, RR - TILE), where, :] = rest.reshape(RR - TILE, TILE, width)
    else:
        rows = part.shape[0] // TILE
        part = jnp.where(own, part, 0.0).astype(BF16)
        out[pl.ds(top * (RR - rows), rows), where, :] = part.reshape(rows, TILE, width)


def first_chunk(chunks, height, asg, feats, wr_h, we_h, ws_h, wb_h, out, xs, wr, we, ws, wb, flags, sems):
    steps = [[]]
    steps[0].append((asg, flags))
    at = 0
    later = []
    for i, chunk in enumerate(chunks):
        moves = [
            (feats.at[tr, col, pl.ds(first, count), :], xs.at[pl.ds(at + row, count), :])
            for tr, col, first, count, row in sources(chunk, top_of(chunk[2]))
        ]
        at += span(chunk, height) * len(columns_of(chunk))
        if i == 0:
            steps[0] += moves
        else:
            later += moves
    steps[0].append((wr_h, wr))
    ends = [sum(WAITS[: i + 1]) for i in range(len(WAITS))]
    first_of = {}
    for i, n_blocks in enumerate(WAITS):
        first_of[1 + ends[i] - n_blocks] = 1 + i
        cols = pl.ds((ends[i] - n_blocks) * BLOCK, n_blocks * BLOCK)
        steps.append(
            [(ws_h.at[:, cols], ws.at[:, cols]), (we_h.at[:, cols], we.at[:, cols]), (wb_h.at[cols, :], wb.at[cols, :])]
        )
    n_weights = len(steps)
    steps.append(later)
    copies = []
    used = 0
    for step in steps:
        copies.append([pltpu.make_async_copy(src, dst, sems.at[used + j]) for j, (src, dst) in enumerate(step)])
        used += len(step)

    def begin(k):
        if k < len(copies):
            for copy in copies[k]:
                copy.start()

    def ready(k):
        for copy in copies[k]:
            copy.wait()
        begin(k + DEPTH)

    for k in range(DEPTH):
        begin(k)
    ready(0)
    per = span(chunks[0], height)
    cols = columns_of(chunks[0])
    reduced = trunk_rows(xs[0 : per * len(cols), :], wr, we, ws, wb, lambda k: ready(first_of[k]) if k in first_of else None)
    for j, col in enumerate(cols):
        put_column(reduced[j * per : (j + 1) * per], chunks[0], col, j, top_of(chunks[0][2]), flags, out)
    for k in range(n_weights, len(copies)):
        ready(k)


def later_chunk(chunk, at, height, flags, xs, wr, we, ws, wb, *refs):
    out = refs[-1]
    top = top_of(chunk[2])
    per = span(chunk, height)
    cols = columns_of(chunk)

    def busy(col):
        own = flags[top, col] >= 0
        if chunk[1]:
            own = own | (flags[1 - top, col] >= 0)
        return own

    active = [busy(col) for col in cols]
    every = functools.reduce(lambda a, b: a & b, active)
    zero = jnp.zeros((span(chunk, height), out.shape[-1]), F32)

    @pl.when(every)
    def _():
        reduced = trunk_rows(xs[at : at + per * len(cols), :], wr, we, ws, wb)
        for j, col in enumerate(cols):
            put_column(reduced[j * per : (j + 1) * per], chunk, col, j, top, flags, out)

    if len(cols) == 1:
        @pl.when(jnp.logical_not(every))
        def _():
            put_column(zero, chunk, cols[0], 0, top, flags, out)
    else:
        for j, col in enumerate(cols):
            @pl.when(jnp.logical_not(active[j]))
            def _():
                put_column(zero, chunk, col, j, top, flags, out)

        one = cols[0]
        step = cols[1] - cols[0]

        @pl.loop(0, len(cols))
        def _(j):
            col = one + j * step
            mine = flags[top, col] >= 0
            if chunk[1]:
                mine = mine | (flags[1 - top, col] >= 0)

            @pl.when(mine & jnp.logical_not(every))
            def _():
                rows = pl.ds(pl.multiple_of(at + j * per, TILE), per)
                put_column(trunk_rows(xs[rows, :], wr, we, ws, wb), chunk, col, j, top, flags, out)

    if not chunk[1]:
        near = refs[0]
        shared = 2 * RR - height
        out[pl.ds((1 - top) * (RR - shared), shared)] = near[pl.ds(top * (RR - shared), shared)]


def pick_kernel(cols_n, used, *refs):
    outs = refs[-(1 if cols_n == 2 else 2) :]
    width = refs[0].shape[1]
    for i, src in enumerate(refs[:used]):
        rows = pl.ds(i * RR, RR)
        if cols_n == 2:
            first = pl.multiple_of((1 - lax.axis_index("col")) * (width - TILE), TILE)
            outs[0][rows] = src[:, pl.ds(first, TILE), :]
        else:
            outs[0][rows] = src[:, width - TILE :, :]
            outs[1][rows] = src[:, :TILE, :]


def place(cols, src, first, count, ext, row, on=None):
    for j, col in enumerate(cols):
        there = src[pl.ds(first, count), j * TILE : (j + 1) * TILE, :]
        if on is not None:
            there = jnp.where(on, there, jnp.zeros_like(there))
        ext[pl.ds(row, count), (1 + col) * TILE : (2 + col) * TILE, :] = there


def place_sides(cols_n, sides, part, first, count, ext, row, on=None):
    me = lax.axis_index("col")
    wide = ext.shape[1]
    for here, at, ref in ((me > 0, 0, sides[0]), (me < cols_n - 1, wide - TILE, sides[-1])):
        there = ref[pl.ds(part * RR + first, count)]
        here = here if on is None else here & on
        ext[pl.ds(row, count), at : at + TILE, :] = jnp.where(here, there, jnp.zeros_like(there))


def spread(ext, cat, width):
    br = ext.shape[-1]
    for b in range(3):
        left = TILE - RC + b * RC
        cat[:, :, b * br : (b + 1) * br] = ext[:, left : left + width, :]


def conv_early(groups, rows_n, cols_n, height, w, *refs):
    g = len(groups)
    ones, twos, far = refs[:g], refs[g : 2 * g], refs[2 * g : 3 * g]
    sides = refs[3 * g : -6]
    out, partial, ext, cat, done, sem = refs[-6:]
    width = cat.shape[1]
    br = ext.shape[2]
    rest = height - RR
    far_top = 1 - near_is_top()
    local = far_top * RR
    for i, (cols, near_first) in enumerate(groups):
        up = top_of(near_first)
        skip = up * (RR - rest)
        rows = [(0, ones[i], 0, RR, local + (1 - up) * rest, None), (1, twos[i], skip, rest, local + up * RR, None)]
        rows += [(2, far[i], 0, RR, (1 - far_top) * height, far_inside(rows_n))]
        for part, src, first, count, row, on in rows:
            place(cols, src, first, count, ext, row, on)
            if i == 0:
                place_sides(cols_n, sides, part, first, count, ext, row, on)
    spread(ext, cat, width)
    k = cat.shape[2]
    total = None
    for a in range(3):
        taps = cat[a * RR : a * RR + rest].reshape(rest * width, k)
        term = jnp.dot(taps, w[a * k : (a + 1) * k, :], preferred_element_type=F32)
        total = term if total is None else total + term
    done[...] = jnp.maximum(total, 0).astype(BF16).reshape(rest, width, br)
    copy = pltpu.make_async_copy(done, out.at[pl.ds((1 - far_top) * RR, rest)], sem)
    copy.start()
    centre = cat[pl.ds(far_top * height, RR)].reshape(RR * width, k)
    inner = cat[pl.ds(far_top * rest + (1 - far_top) * RR, RR)].reshape(RR * width, k)
    inner_w = w[pl.ds(pl.multiple_of((1 - far_top) * 2 * k, k), k), :]
    total = jnp.dot(centre, w[k : 2 * k, :], preferred_element_type=F32) + jnp.dot(
        inner, inner_w, preferred_element_type=F32
    )
    partial[...] = total.reshape(RR, width, br)
    copy.wait()


def far_inside(rows_n):
    me = lax.axis_index("row")
    return (me > 0) & (me < rows_n - 1)


def products(halo, cols, w, taps, base, apart):
    top = near_is_top()
    value = halo[...]
    rows, wide, br = value.shape
    for b in taps:
        tap = w[pl.ds(pl.multiple_of((6 * (1 - top) + b) * br, br), br), :]
        term = jnp.dot(value.reshape(rows * wide, br), tap, preferred_element_type=F32).reshape(rows, wide, br)
        for j, col in enumerate(cols):
            at = (1 + col) * TILE - base
            apart[b, :, at : at + TILE, :] = term[:, j * TILE : (j + 1) * TILE, :]


def conv_mid(groups, cols_n, w, partial, near, *refs):
    sides = refs[:-3]
    out, apart, rim = refs[-3:]
    width, br = partial.shape[1:]
    tile_cols = width // TILE
    for cols, _ in groups[1:]:
        for col in cols:
            for b in range(3):
                apart[b, :, (1 + col) * TILE : (2 + col) * TILE, :] = jnp.zeros((RR, TILE, br), F32)
    products(near, groups[0][0], w, range(3), 0, apart)
    me = lax.axis_index("col")
    for on, b, col, ref in ((me > 0, 0, -1, sides[0]), (me < cols_n - 1, 2, tile_cols, sides[-1])):
        there = ref[...]
        rim[...] = jnp.where(on, there, jnp.zeros_like(there))
        products(rim, [col], w, [b], 0, apart)
    for at in range(0, RR, 6):
        rows = slice(at, min(at + 6, RR))
        total = partial[rows]
        for b in range(3):
            left = TILE - RC + b * RC
            total = total + apart[b, rows, left : left + width, :]
        out[rows] = total


def conv_late(groups, height, w, partial, *refs):
    near = refs[: len(groups) - 1]
    _, out, apart, done, sems = refs[-5:]
    top = near_is_top()
    width, br = partial.shape[1:]
    rest = height - RR
    used = sorted(col for cols, _ in groups[1:] for col in cols)
    lo, hi = used[0] * TILE, (used[-1] + 1) * TILE
    reach = []
    for b in range(3):
        shift = (b - 1) * RC
        reach.append((max(0, lo - shift) // TILE * TILE, min(width, -(-(hi - shift) // TILE) * TILE)))
    cuts = sorted({0, width, *[edge for span_b in reach for edge in span_b]})
    zero = jnp.zeros((RR, TILE, br), F32)
    for b in range(3):
        apart[b, :, 0:TILE, :] = zero
        apart[b, :, TILE + hi - lo : 2 * TILE + hi - lo, :] = zero
    for i, (cols, _) in enumerate(groups[1:]):
        products(near[i], cols, w, range(3), lo, apart)
    copies = []
    step = RR // LATE
    for at in range(0, RR, step):
        for left, right in zip(cuts, cuts[1:]):
            total = partial[at : at + step, left:right, :]
            for b in range(3):
                if reach[b][0] <= left and right <= reach[b][1]:
                    first = left + (b - 1) * RC + TILE - lo
                    total = total + apart[b, at : at + step, first : first + right - left, :]
            done[at : at + step, left:right, :] = jnp.maximum(total, 0).astype(BF16)
        there = out.at[pl.ds((1 - top) * rest + at, step)]
        copies.append(pltpu.make_async_copy(done.at[pl.ds(at, step)], there, sems.at[len(copies)]))
        copies[-1].start()
    for copy in copies:
        copy.wait()


def plan(tile_cols):
    groups = [([0, tile_cols - 1], False), (list(range(1, tile_cols - 1)), False)]
    order = [(0, True), (0, False), (1, True), (1, False)]
    return groups, order


def shards(features, assignment, w_reduce, w_expand, w_short, w_branch, w_dilated):
    tile_rows, tile_cols, pixels, channels = features.shape
    mid, cout, br = w_reduce.shape[1], w_expand.shape[1], w_branch.shape[1]
    height, width = tile_rows * TILE, tile_cols * TILE
    assert tile_rows == 2 and pixels == TILE * TILE and TILE < RR <= height <= 2 * RR
    groups, order = plan(tile_cols)
    chunks = [(groups[i][0], one, groups[i][1]) for i, one in order]
    sizes = [span(c, height) * len(c[0]) for c in chunks]
    starts = [sum(sizes[:i]) for i in range(len(sizes))]
    per_row = 2 * (channels * mid + mid * cout + channels * cout + cout * br)
    n_copies = sum(len(list(sources(c, 0))) for c in chunks) + 2 + 3 * (cout // BLOCK)

    def grid_of(cols):
        return jax.ShapeDtypeStruct((RR, len(cols) * TILE, br), BF16)

    first, xs, wr, we, ws, wb = pl.pallas_call(
        functools.partial(first_chunk, chunks, height),
        out_shape=[
            grid_of(chunks[0][0]),
            jax.ShapeDtypeStruct((sum(sizes), channels), BF16),
            jax.ShapeDtypeStruct(w_reduce.shape, BF16),
            jax.ShapeDtypeStruct(w_expand.shape, BF16),
            jax.ShapeDtypeStruct(w_short.shape, BF16),
            jax.ShapeDtypeStruct(w_branch.shape, BF16),
        ],
        in_specs=[HBM] * 6,
        out_specs=[VM] * 6,
        scratch_shapes=[pltpu.SMEM(assignment.shape, jnp.int32), pltpu.SemaphoreType.DMA((n_copies,))],
        compiler_params=params(TRUNK_MIB),
        cost_estimate=cost(per_row * sizes[0], 12 * MIB),
        name="trunk_first",
    )(*[in_hbm(v) for v in (assignment, features, w_reduce, w_expand, w_short, w_branch)])

    rows_n, cols_n = lax.axis_size("row"), lax.axis_size("col")
    assert rows_n % 2 == 0 and cols_n % 2 == 0

    def partner(row, col, near):
        if near:
            return row ^ 1, col
        if row in (0, rows_n - 1):
            return row, col ^ 1
        return (row + 1 if row % 2 else row - 1), col

    def swap(near):
        pairs = []
        for row in range(rows_n):
            for col in range(cols_n):
                to_row, to_col = partner(row, col, near)
                pairs.append((row * cols_n + col, to_row * cols_n + to_col))
        return pairs

    local, halo = {}, {}
    for n, (i, one) in enumerate(order):
        if n == 0:
            value = first
        else:
            extra = [] if one else [local[i, True]]
            value = pl.pallas_call(
                functools.partial(later_chunk, chunks[n], starts[n], height),
                out_shape=grid_of(groups[i][0]),
                in_specs=[SM] + [VM] * (5 + len(extra)),
                out_specs=VM,
                compiler_params=params(TRUNK_MIB),
                cost_estimate=cost(per_row * sizes[n], MIB),
            )(assignment, xs, wr, we, ws, wb, *extra)
        local[i, one] = value
        near = one == groups[i][1]
        halo[i, near] = lax.ppermute(value, ("row", "col"), swap(near))

    def trade(arrays, after=()):
        used = len(arrays)
        side = jax.ShapeDtypeStruct((used * RR, TILE, br), BF16)
        n_out = 1 if cols_n == 2 else 2
        picked = pl.pallas_call(
            functools.partial(pick_kernel, cols_n, used),
            out_shape=[side] * n_out,
            in_specs=[VM] * used + [pl.BlockSpec(memory_space=pl.ANY)] * len(after),
            out_specs=[VM] * n_out,
            compiler_params=params(4),
            cost_estimate=cost(0, MIB),
        )(*arrays, *after)
        if cols_n == 2:
            return [lax.ppermute(picked[0], "col", [(0, 1), (1, 0)])]
        return [
            lax.ppermute(picked[0], "col", [(i, i + 1) for i in range(cols_n - 1)]),
            lax.ppermute(picked[1], "col", [(i + 1, i) for i in range(cols_n - 1)]),
        ]

    taps = w_dilated.reshape(9 * br, br)
    rest = height - RR
    n_groups = len(groups)
    pick = lambda table, key: [table[i, key] for i in range(n_groups)]
    flops = 2 * width * 3 * br * br
    sides = trade([local[0, True], local[0, False], halo[0, False]])
    out, partial = pl.pallas_call(
        functools.partial(conv_early, groups, rows_n, cols_n, height),
        out_shape=[
            jax.ShapeDtypeStruct((height, width, br), BF16),
            jax.ShapeDtypeStruct((RR, width, br), F32),
        ],
        in_specs=[VM] * (1 + 3 * n_groups + len(sides)),
        out_specs=[HBM, VM],
        scratch_shapes=[
            pltpu.VMEM((height + RR, width + 2 * TILE, br), BF16),
            pltpu.VMEM((height + RR, width, 3 * br), BF16),
            pltpu.VMEM((rest, width, br), BF16),
            pltpu.SemaphoreType.DMA,
        ],
        compiler_params=params(CONV_MIB),
        cost_estimate=cost(flops * (3 * rest + 2 * RR), 4 * MIB),
        name="conv_early",
    )(taps, *pick(local, True), *pick(local, False), *pick(halo, False), *sides)
    rims = trade([halo[0, True]], [partial])
    partial = pl.pallas_call(
        functools.partial(conv_mid, groups, cols_n),
        out_shape=jax.ShapeDtypeStruct((RR, width, br), F32),
        in_specs=[VM] * (3 + len(rims)),
        out_specs=VM,
        scratch_shapes=[
            pltpu.VMEM((3, RR, width + 2 * TILE, br), F32),
            pltpu.VMEM((RR, TILE, br), BF16),
        ],
        compiler_params=params(16),
        cost_estimate=cost(flops * RR, 4 * MIB),
        name="conv_mid",
    )(taps, partial, halo[0, True], *rims)
    inner = sum(len(cols) for cols, _ in groups[1:]) * TILE
    n_in = 1 + n_groups
    return pl.pallas_call(
        functools.partial(conv_late, groups, height),
        out_shape=jax.ShapeDtypeStruct((height, width, br), BF16),
        in_specs=[VM] * n_in + [HBM],
        out_specs=HBM,
        input_output_aliases={n_in: 0},
        scratch_shapes=[
            pltpu.VMEM((3, RR, inner + 2 * TILE, br), F32),
            pltpu.VMEM((RR, width, br), BF16),
            pltpu.SemaphoreType.DMA((LATE,)),
        ],
        compiler_params=params(16),
        cost_estimate=cost(flops * RR, 4 * MIB),
        name="conv_late",
    )(taps, partial, *pick(halo, True)[1:], out)


def solution(mesh):
    in_specs = (
        P(("groups", "row"), "col", None, None),
        P(("groups", "row"), "col"),
        P(),
        P(),
        P(),
        P(),
        P(),
    )
    out_specs = P(("groups", "row"), "col", None)

    return jax.shard_map(shards, mesh=mesh, in_specs=in_specs, out_specs=out_specs, check_vma=False)
```

```python
import functools

import jax
import jax.numpy as jnp
from jax import lax
from jax.experimental import pallas as pl
from jax.experimental.pallas import tpu as pltpu
from jax.sharding import PartitionSpec as P


TILE = 16
RR = 18
RC = 15
BLOCK = 512
DEPTH = 3
WAITS = (1, 3)
LATE = 1
F32 = jnp.float32
BF16 = jnp.bfloat16
VM = pl.BlockSpec(memory_space=pltpu.VMEM)
SM = pl.BlockSpec(memory_space=pltpu.SMEM)
HBM = pl.BlockSpec(memory_space=pltpu.MemorySpace.HBM)
MIB = 1 << 20
TRUNK_MIB = 16
CONV_MIB = 24


def params(mib):
    return pltpu.CompilerParams(vmem_limit_bytes=mib * MIB)


def cost(flops, nbytes):
    return pl.CostEstimate(flops=int(flops), bytes_accessed=int(nbytes), transcendentals=0)


def in_hbm(value):
    return pltpu.with_memory_space_constraint(value, pltpu.MemorySpace.HBM)


def near_is_top():
    return lax.rem(lax.axis_index("row"), 2)


def top_of(near_first):
    return near_is_top() if near_first else 1 - near_is_top()


def columns_of(chunk):
    return chunk[0]


def span(chunk, height):
    return (RR if chunk[1] else height - RR) * TILE


def sources(chunk, top):
    rest = (RR - TILE) * TILE
    pixels = TILE * TILE
    for j, col in enumerate(chunk[0]):
        if chunk[1]:
            at = j * (pixels + rest)
            yield 1 - top, col, 0, pixels, at
            yield top, col, (1 - top) * (pixels - rest), rest, at + pixels
        else:
            yield top, col, top * rest, pixels - rest, j * (pixels - rest)


def trunk_rows(x, wr, we, ws, wb, ready=lambda k: None):
    ready(0)
    hidden = jnp.maximum(jnp.dot(x, wr[...], preferred_element_type=F32), 0).astype(BF16)
    total = None
    for k, at in enumerate(range(0, we.shape[1], BLOCK)):
        ready(1 + k)
        summed = jnp.dot(hidden, we[:, at : at + BLOCK], preferred_element_type=F32)
        summed = summed + jnp.dot(x, ws[:, at : at + BLOCK], preferred_element_type=F32)
        block_out = jnp.maximum(summed, 0).astype(BF16)
        term = jnp.dot(block_out, wb[at : at + BLOCK, :], preferred_element_type=F32)
        total = term if total is None else total + term
    return jnp.maximum(total, 0)


def put_column(part, chunk, col, j, top, flags, out):
    width = part.shape[-1]
    where = pl.ds(j * TILE, TILE)
    own = flags[top, col] >= 0
    if chunk[1]:
        pixels = TILE * TILE
        full = jnp.where(flags[1 - top, col] >= 0, part[:pixels], 0.0).astype(BF16)
        rest = jnp.where(own, part[pixels:], 0.0).astype(BF16)
        out[pl.ds((1 - top) * (RR - TILE), TILE), where, :] = full.reshape(TILE, TILE, width)
        out[pl.ds(top * TILE, RR - TILE), where, :] = rest.reshape(RR - TILE, TILE, width)
    else:
        rows = part.shape[0] // TILE
        part = jnp.where(own, part, 0.0).astype(BF16)
        out[pl.ds(top * (RR - rows), rows), where, :] = part.reshape(rows, TILE, width)


def first_chunk(chunks, height, asg, feats, wr_h, we_h, ws_h, wb_h, out, xs, wr, we, ws, wb, flags, sems):
    steps = [[]]
    steps[0].append((asg, flags))
    at = 0
    later = []
    for i, chunk in enumerate(chunks):
        moves = [
            (feats.at[tr, col, pl.ds(first, count), :], xs.at[pl.ds(at + row, count), :])
            for tr, col, first, count, row in sources(chunk, top_of(chunk[2]))
        ]
        at += span(chunk, height) * len(columns_of(chunk))
        if i == 0:
            steps[0] += moves
        else:
            later += moves
    steps[0].append((wr_h, wr))
    ends = [sum(WAITS[: i + 1]) for i in range(len(WAITS))]
    first_of = {}
    for i, n_blocks in enumerate(WAITS):
        first_of[1 + ends[i] - n_blocks] = 1 + i
        cols = pl.ds((ends[i] - n_blocks) * BLOCK, n_blocks * BLOCK)
        steps.append(
            [(ws_h.at[:, cols], ws.at[:, cols]), (we_h.at[:, cols], we.at[:, cols]), (wb_h.at[cols, :], wb.at[cols, :])]
        )
    n_weights = len(steps)
    steps.append(later)
    copies = []
    used = 0
    for step in steps:
        copies.append([pltpu.make_async_copy(src, dst, sems.at[used + j]) for j, (src, dst) in enumerate(step)])
        used += len(step)

    def begin(k):
        if k < len(copies):
            for copy in copies[k]:
                copy.start()

    def ready(k):
        for copy in copies[k]:
            copy.wait()
        begin(k + DEPTH)

    for k in range(DEPTH):
        begin(k)
    ready(0)
    per = span(chunks[0], height)
    cols = columns_of(chunks[0])
    reduced = trunk_rows(xs[0 : per * len(cols), :], wr, we, ws, wb, lambda k: ready(first_of[k]) if k in first_of else None)
    for j, col in enumerate(cols):
        put_column(reduced[j * per : (j + 1) * per], chunks[0], col, j, top_of(chunks[0][2]), flags, out)
    for k in range(n_weights, len(copies)):
        ready(k)


def later_chunk(chunk, at, height, flags, xs, wr, we, ws, wb, *refs):
    out = refs[-1]
    top = top_of(chunk[2])
    per = span(chunk, height)
    cols = columns_of(chunk)

    def busy(col):
        own = flags[top, col] >= 0
        if chunk[1]:
            own = own | (flags[1 - top, col] >= 0)
        return own

    active = [busy(col) for col in cols]
    every = functools.reduce(lambda a, b: a & b, active)
    zero = jnp.zeros((span(chunk, height), out.shape[-1]), F32)

    @pl.when(every)
    def _():
        reduced = trunk_rows(xs[at : at + per * len(cols), :], wr, we, ws, wb)
        for j, col in enumerate(cols):
            put_column(reduced[j * per : (j + 1) * per], chunk, col, j, top, flags, out)

    if len(cols) == 1:
        @pl.when(jnp.logical_not(every))
        def _():
            put_column(zero, chunk, cols[0], 0, top, flags, out)
    else:
        for j, col in enumerate(cols):
            @pl.when(jnp.logical_not(active[j]))
            def _():
                put_column(zero, chunk, col, j, top, flags, out)

        one = cols[0]
        step = cols[1] - cols[0]

        @pl.loop(0, len(cols))
        def _(j):
            col = one + j * step
            mine = flags[top, col] >= 0
            if chunk[1]:
                mine = mine | (flags[1 - top, col] >= 0)

            @pl.when(mine & jnp.logical_not(every))
            def _():
                rows = pl.ds(pl.multiple_of(at + j * per, TILE), per)
                put_column(trunk_rows(xs[rows, :], wr, we, ws, wb), chunk, col, j, top, flags, out)

    if not chunk[1]:
        near = refs[0]
        shared = 2 * RR - height
        out[pl.ds((1 - top) * (RR - shared), shared)] = near[pl.ds(top * (RR - shared), shared)]


def pick_kernel(cols_n, used, *refs):
    outs = refs[-(1 if cols_n == 2 else 2) :]
    width = refs[0].shape[1]
    for i, src in enumerate(refs[:used]):
        rows = pl.ds(i * RR, RR)
        if cols_n == 2:
            first = pl.multiple_of((1 - lax.axis_index("col")) * (width - TILE), TILE)
            outs[0][rows] = src[:, pl.ds(first, TILE), :]
        else:
            outs[0][rows] = src[:, width - TILE :, :]
            outs[1][rows] = src[:, :TILE, :]


def place(cols, src, first, count, ext, row, on=None):
    for j, col in enumerate(cols):
        there = src[pl.ds(first, count), j * TILE : (j + 1) * TILE, :]
        if on is not None:
            there = jnp.where(on, there, jnp.zeros_like(there))
        ext[pl.ds(row, count), (1 + col) * TILE : (2 + col) * TILE, :] = there


def place_sides(cols_n, sides, part, first, count, ext, row, on=None):
    me = lax.axis_index("col")
    wide = ext.shape[1]
    for here, at, ref in ((me > 0, 0, sides[0]), (me < cols_n - 1, wide - TILE, sides[-1])):
        there = ref[pl.ds(part * RR + first, count)]
        here = here if on is None else here & on
        ext[pl.ds(row, count), at : at + TILE, :] = jnp.where(here, there, jnp.zeros_like(there))


def spread(ext, cat, width):
    br = ext.shape[-1]
    for b in range(3):
        left = TILE - RC + b * RC
        cat[:, :, b * br : (b + 1) * br] = ext[:, left : left + width, :]


def conv_early(groups, rows_n, cols_n, height, w, *refs):
    g = len(groups)
    ones, twos, far = refs[:g], refs[g : 2 * g], refs[2 * g : 3 * g]
    sides = refs[3 * g : -6]
    out, partial, ext, cat, done, sem = refs[-6:]
    width = cat.shape[1]
    br = ext.shape[2]
    rest = height - RR
    far_top = 1 - near_is_top()
    local = far_top * RR
    for i, (cols, near_first) in enumerate(groups):
        up = top_of(near_first)
        skip = up * (RR - rest)
        rows = [(0, ones[i], 0, RR, local + (1 - up) * rest, None), (1, twos[i], skip, rest, local + up * RR, None)]
        rows += [(2, far[i], 0, RR, (1 - far_top) * height, far_inside(rows_n))]
        for part, src, first, count, row, on in rows:
            place(cols, src, first, count, ext, row, on)
            if i == 0:
                place_sides(cols_n, sides, part, first, count, ext, row, on)
    spread(ext, cat, width)
    k = cat.shape[2]
    total = None
    for a in range(3):
        taps = cat[a * RR : a * RR + rest].reshape(rest * width, k)
        term = jnp.dot(taps, w[a * k : (a + 1) * k, :], preferred_element_type=F32)
        total = term if total is None else total + term
    done[...] = jnp.maximum(total, 0).astype(BF16).reshape(rest, width, br)
    copy = pltpu.make_async_copy(done, out.at[pl.ds((1 - far_top) * RR, rest)], sem)
    copy.start()
    centre = cat[pl.ds(far_top * height, RR)].reshape(RR * width, k)
    inner = cat[pl.ds(far_top * rest + (1 - far_top) * RR, RR)].reshape(RR * width, k)
    inner_w = w[pl.ds(pl.multiple_of((1 - far_top) * 2 * k, k), k), :]
    total = jnp.dot(centre, w[k : 2 * k, :], preferred_element_type=F32) + jnp.dot(
        inner, inner_w, preferred_element_type=F32
    )
    partial[...] = total.reshape(RR, width, br)
    copy.wait()


def far_inside(rows_n):
    me = lax.axis_index("row")
    return (me > 0) & (me < rows_n - 1)


def products(halo, cols, w, taps, base, apart):
    top = near_is_top()
    value = halo[...]
    rows, wide, br = value.shape
    for b in taps:
        tap = w[pl.ds(pl.multiple_of((6 * (1 - top) + b) * br, br), br), :]
        term = jnp.dot(value.reshape(rows * wide, br), tap, preferred_element_type=F32).reshape(rows, wide, br)
        for j, col in enumerate(cols):
            at = (1 + col) * TILE - base
            apart[b, :, at : at + TILE, :] = term[:, j * TILE : (j + 1) * TILE, :]


def conv_mid(groups, cols_n, w, partial, near, *refs):
    sides = refs[:-3]
    out, apart, rim = refs[-3:]
    width, br = partial.shape[1:]
    tile_cols = width // TILE
    for cols, _ in groups[1:]:
        for col in cols:
            for b in range(3):
                apart[b, :, (1 + col) * TILE : (2 + col) * TILE, :] = jnp.zeros((RR, TILE, br), F32)
    products(near, groups[0][0], w, range(3), 0, apart)
    me = lax.axis_index("col")
    for on, b, col, ref in ((me > 0, 0, -1, sides[0]), (me < cols_n - 1, 2, tile_cols, sides[-1])):
        there = ref[...]
        rim[...] = jnp.where(on, there, jnp.zeros_like(there))
        products(rim, [col], w, [b], 0, apart)
    for at in range(0, RR, 6):
        rows = slice(at, min(at + 6, RR))
        total = partial[rows]
        for b in range(3):
            left = TILE - RC + b * RC
            total = total + apart[b, rows, left : left + width, :]
        out[rows] = total


def conv_late(groups, height, w, partial, *refs):
    near = refs[: len(groups) - 1]
    _, out, apart, done, sems = refs[-5:]
    top = near_is_top()
    width, br = partial.shape[1:]
    rest = height - RR
    used = sorted(col for cols, _ in groups[1:] for col in cols)
    lo, hi = used[0] * TILE, (used[-1] + 1) * TILE
    reach = []
    for b in range(3):
        shift = (b - 1) * RC
        reach.append((max(0, lo - shift) // TILE * TILE, min(width, -(-(hi - shift) // TILE) * TILE)))
    cuts = sorted({0, width, *[edge for span_b in reach for edge in span_b]})
    zero = jnp.zeros((RR, TILE, br), F32)
    for b in range(3):
        apart[b, :, 0:TILE, :] = zero
        apart[b, :, TILE + hi - lo : 2 * TILE + hi - lo, :] = zero
    for i, (cols, _) in enumerate(groups[1:]):
        products(near[i], cols, w, range(3), lo, apart)
    copies = []
    step = RR // LATE
    for at in range(0, RR, step):
        for left, right in zip(cuts, cuts[1:]):
            total = partial[at : at + step, left:right, :]
            for b in range(3):
                if reach[b][0] <= left and right <= reach[b][1]:
                    first = left + (b - 1) * RC + TILE - lo
                    total = total + apart[b, at : at + step, first : first + right - left, :]
            done[at : at + step, left:right, :] = jnp.maximum(total, 0).astype(BF16)
        there = out.at[pl.ds((1 - top) * rest + at, step)]
        copies.append(pltpu.make_async_copy(done.at[pl.ds(at, step)], there, sems.at[len(copies)]))
        copies[-1].start()
    for copy in copies:
        copy.wait()


def plan(tile_cols):
    groups = [([0, tile_cols - 1], True), (list(range(1, tile_cols - 1)), False)]
    order = [(0, True), (0, False), (1, True), (1, False)]
    return groups, order


def shards(features, assignment, w_reduce, w_expand, w_short, w_branch, w_dilated):
    tile_rows, tile_cols, pixels, channels = features.shape
    mid, cout, br = w_reduce.shape[1], w_expand.shape[1], w_branch.shape[1]
    height, width = tile_rows * TILE, tile_cols * TILE
    assert tile_rows == 2 and pixels == TILE * TILE and TILE < RR <= height <= 2 * RR
    groups, order = plan(tile_cols)
    chunks = [(groups[i][0], one, groups[i][1]) for i, one in order]
    sizes = [span(c, height) * len(c[0]) for c in chunks]
    starts = [sum(sizes[:i]) for i in range(len(sizes))]
    per_row = 2 * (channels * mid + mid * cout + channels * cout + cout * br)
    n_copies = sum(len(list(sources(c, 0))) for c in chunks) + 2 + 3 * (cout // BLOCK)

    def grid_of(cols):
        return jax.ShapeDtypeStruct((RR, len(cols) * TILE, br), BF16)

    first, xs, wr, we, ws, wb = pl.pallas_call(
        functools.partial(first_chunk, chunks, height),
        out_shape=[
            grid_of(chunks[0][0]),
            jax.ShapeDtypeStruct((sum(sizes), channels), BF16),
            jax.ShapeDtypeStruct(w_reduce.shape, BF16),
            jax.ShapeDtypeStruct(w_expand.shape, BF16),
            jax.ShapeDtypeStruct(w_short.shape, BF16),
            jax.ShapeDtypeStruct(w_branch.shape, BF16),
        ],
        in_specs=[HBM] * 6,
        out_specs=[VM] * 6,
        scratch_shapes=[pltpu.SMEM(assignment.shape, jnp.int32), pltpu.SemaphoreType.DMA((n_copies,))],
        compiler_params=params(TRUNK_MIB),
        cost_estimate=cost(per_row * sizes[0], 12 * MIB),
        name="trunk_first",
    )(*[in_hbm(v) for v in (assignment, features, w_reduce, w_expand, w_short, w_branch)])

    rows_n, cols_n = lax.axis_size("row"), lax.axis_size("col")
    assert rows_n % 2 == 0 and cols_n % 2 == 0

    def partner(row, col, near):
        if near:
            return row ^ 1, col
        if row in (0, rows_n - 1):
            return row, col ^ 1
        return (row + 1 if row % 2 else row - 1), col

    def swap(near):
        pairs = []
        for row in range(rows_n):
            for col in range(cols_n):
                to_row, to_col = partner(row, col, near)
                pairs.append((row * cols_n + col, to_row * cols_n + to_col))
        return pairs

    local, halo = {}, {}
    for n, (i, one) in enumerate(order):
        if n == 0:
            value = first
        else:
            extra = [] if one else [local[i, True]]
            value = pl.pallas_call(
                functools.partial(later_chunk, chunks[n], starts[n], height),
                out_shape=grid_of(groups[i][0]),
                in_specs=[SM] + [VM] * (5 + len(extra)),
                out_specs=VM,
                compiler_params=params(TRUNK_MIB),
                cost_estimate=cost(per_row * sizes[n], MIB),
            )(assignment, xs, wr, we, ws, wb, *extra)
        local[i, one] = value
        near = one == groups[i][1]
        halo[i, near] = lax.ppermute(value, ("row", "col"), swap(near))

    def trade(arrays):
        used = len(arrays)
        side = jax.ShapeDtypeStruct((used * RR, TILE, br), BF16)
        n_out = 1 if cols_n == 2 else 2
        picked = pl.pallas_call(
            functools.partial(pick_kernel, cols_n, used),
            out_shape=[side] * n_out,
            in_specs=[VM] * used,
            out_specs=[VM] * n_out,
            compiler_params=params(4),
            cost_estimate=cost(0, MIB),
        )(*arrays)
        if cols_n == 2:
            return [lax.ppermute(picked[0], "col", [(0, 1), (1, 0)])]
        return [
            lax.ppermute(picked[0], "col", [(i, i + 1) for i in range(cols_n - 1)]),
            lax.ppermute(picked[1], "col", [(i + 1, i) for i in range(cols_n - 1)]),
        ]

    taps = w_dilated.reshape(9 * br, br)
    rest = height - RR
    n_groups = len(groups)
    pick = lambda table, key: [table[i, key] for i in range(n_groups)]
    flops = 2 * width * 3 * br * br
    sides = trade([local[0, True], local[0, False], halo[0, False]])
    out, partial = pl.pallas_call(
        functools.partial(conv_early, groups, rows_n, cols_n, height),
        out_shape=[
            jax.ShapeDtypeStruct((height, width, br), BF16),
            jax.ShapeDtypeStruct((RR, width, br), F32),
        ],
        in_specs=[VM] * (1 + 3 * n_groups + len(sides)),
        out_specs=[HBM, VM],
        scratch_shapes=[
            pltpu.VMEM((height + RR, width + 2 * TILE, br), BF16),
            pltpu.VMEM((height + RR, width, 3 * br), BF16),
            pltpu.VMEM((rest, width, br), BF16),
            pltpu.SemaphoreType.DMA,
        ],
        compiler_params=params(CONV_MIB),
        cost_estimate=cost(flops * (3 * rest + 2 * RR), 4 * MIB),
        name="conv_early",
    )(taps, *pick(local, True), *pick(local, False), *pick(halo, False), *sides)
    rims = trade([halo[0, True]])
    partial = pl.pallas_call(
        functools.partial(conv_mid, groups, cols_n),
        out_shape=jax.ShapeDtypeStruct((RR, width, br), F32),
        in_specs=[VM] * (3 + len(rims)),
        out_specs=VM,
        scratch_shapes=[
            pltpu.VMEM((3, RR, width + 2 * TILE, br), F32),
            pltpu.VMEM((RR, TILE, br), BF16),
        ],
        compiler_params=params(16),
        cost_estimate=cost(flops * RR, 4 * MIB),
        name="conv_mid",
    )(taps, partial, halo[0, True], *rims)
    inner = sum(len(cols) for cols, _ in groups[1:]) * TILE
    n_in = 1 + n_groups
    return pl.pallas_call(
        functools.partial(conv_late, groups, height),
        out_shape=jax.ShapeDtypeStruct((height, width, br), BF16),
        in_specs=[VM] * n_in + [HBM],
        out_specs=HBM,
        input_output_aliases={n_in: 0},
        scratch_shapes=[
            pltpu.VMEM((3, RR, inner + 2 * TILE, br), F32),
            pltpu.VMEM((RR, width, br), BF16),
            pltpu.SemaphoreType.DMA((LATE,)),
        ],
        compiler_params=params(16),
        cost_estimate=cost(flops * RR, 4 * MIB),
        name="conv_late",
    )(taps, partial, *pick(halo, True)[1:], out)


def solution(mesh):
    in_specs = (
        P(("groups", "row"), "col", None, None),
        P(("groups", "row"), "col"),
        P(),
        P(),
        P(),
        P(),
        P(),
    )
    out_specs = P(("groups", "row"), "col", None)

    return jax.shard_map(shards, mesh=mesh, in_specs=in_specs, out_specs=out_specs, check_vma=False)
```
